32 devices in a mesh: groups: 2 (over x), ctx: 16 (over z, y, core).
Axes of the slice: x: 2, y: 2, z: 4, core: 2. Of those that a mesh axis runs over, the one named last changes fastest.
Arguments:
- query_rows: bfloat16 [16384, 1024], P(('groups', 'ctx')), parts along dimension 0, may hold values from -6 to 6
- key_rows: bfloat16 [16384, 1024], P(('groups', 'ctx')), parts along dimension 0, may hold values from -0.375 to 0.375
- value_rows: bfloat16 [16384, 2048], P(('groups', 'ctx')), parts along dimension 0, may hold values from -6 to 6
- out_grad: bfloat16 [16384, 2048], P(('groups', 'ctx')), parts along dimension 0, may hold values from -0.25 to 0.25
- log_forget: float32 [16384, 4], P(('groups', 'ctx')), parts along dimension 0, may hold values from -0.75 to 0
- input_pre: float32 [16384, 4], P(('groups', 'ctx')), parts along dimension 0, may hold values from -3 to 0.5
- doc_starts: int32 [16384], P(('groups', 'ctx')), parts along dimension 0, may hold values from 0 to 1, as said below
Outputs:
- grad_queries: bfloat16 [16384, 1024], P(('groups', 'ctx')), parts along dimension 0
- grad_keys: bfloat16 [16384, 1024], P(('groups', 'ctx')), parts along dimension 0
- grad_values: bfloat16 [16384, 2048], P(('groups', 'ctx')), parts along dimension 0
The draws below stay inside these ranges and needn't reach their ends.
There are 2 independent parts, one for each index of `groups`. The reference program is written for one: setup_inputs(seed, part) draws one part's arguments, and reference() takes and returns one part's arrays. A program takes and returns all parts, laid end to end along the dimension named above; each array names one. Nothing has to cross between parts.
Inputs may be any that keep to these rules, and one draw needn't show every extreme that they name: doc_starts is 1 at the sequence's first position; every document has at most 2048 positions, and some document has exactly that many.
All inputs are finite; a program needn't handle non-finite values.
Results may differ from the reference program's by a relative error of at most 0.0056.
Values may be sent and summed in bfloat16 or wider, within the bound.
No kernel may reach another device: no remote copies, remote signals or barrier semaphores. Data moves between devices by JAX's collectives and lax.ppermute only.
A program may use at most 192 MiB of HBM per device.

```python
import jax
import jax.numpy as jnp
from jax import lax

HEADS = 4
DK = 256
DV = 512
SPAN_POSITIONS = 512
TEXT_SPAN_COUNT = 4
SEQUENCE_EXTENT = 8192


def draw_log_forget(key, part):
    permute_seed, jitter_seed, cluster_seed, portion_seed = jax.random.split(key, 4)
    ranking = jax.random.permutation(permute_seed, HEADS)
    slow_count = HEADS // 2
    slow_head = ranking < slow_count
    default_probability = jnp.where(slow_head, 0.25 / (TEXT_SPAN_COUNT * SPAN_POSITIONS), 1.0 / 40.0)
    jitter_amplitude = jax.random.uniform(jitter_seed, (SEQUENCE_EXTENT, HEADS), jnp.float32, 0.5, 2.0)
    cluster_aligned = jax.random.uniform(cluster_seed, (SEQUENCE_EXTENT, 1), jnp.float32) < 2.0 / (TEXT_SPAN_COUNT * SPAN_POSITIONS)
    dropped_portion = jax.random.uniform(portion_seed, (SEQUENCE_EXTENT, 1), jnp.float32, 0.2, 0.5)
    return -default_probability[None, :] * jitter_amplitude + jnp.where(cluster_aligned, jnp.log(1.0 - dropped_portion), 0.0)


def draw_doc_starts(key, part):
    length_key, place_key = jax.random.split(key)
    longest = TEXT_SPAN_COUNT * SPAN_POSITIONS
    lengths = jax.random.randint(length_key, (SEQUENCE_EXTENT,), 1, longest + 1)
    lengths = lengths.at[jax.random.randint(place_key, (), 0, 4)].set(longest)
    bounds = jnp.cumsum(lengths) - lengths
    return jnp.zeros((SEQUENCE_EXTENT,), jnp.int32).at[bounds].set(1, mode='drop')


def block_scale(own_key, extent, pieces, low, high):
    factor_of = 1.0
    for dim, shards_of in pieces:
        steps = jax.random.uniform(jax.random.fold_in(jax.random.fold_in(own_key, 6), dim), (shards_of,), jnp.float32, low / len(pieces), high / len(pieces))
        factor_of = factor_of * jnp.repeat(jnp.exp(steps), extent[dim] // shards_of).reshape((-1,) + (1,) * (len(extent) - 1 - dim))
    return factor_of


def bell_draw(key, extent, spread, limit, cuts=(), kind=jnp.bfloat16):
    entries = spread * jax.random.normal(key, extent, jnp.float32)
    if cuts:
        entries = entries * block_scale(key, extent, cuts, -0.22, 0.18)
    return jnp.clip(entries, -limit, limit).astype(kind)


def setup_inputs(seed: int = 0, part: int = 0) -> dict:
    key_list = jax.random.split(jax.random.key(seed), 8)
    part_splits = jax.random.split(jax.random.fold_in(key_list[7], part), 8)
    return {
        "query_rows": bell_draw(part_splits[0], (SEQUENCE_EXTENT, HEADS * DK), 1.0, 6.0, ((0, 16),)),
        "key_rows": bell_draw(part_splits[1], (SEQUENCE_EXTENT, HEADS * DK), DK ** -0.5, 0.375, ((0, 16),)),
        "value_rows": bell_draw(part_splits[2], (SEQUENCE_EXTENT, HEADS * DV), 1.0, 6.0, ((0, 16),)),
        "out_grad": bell_draw(part_splits[3], (SEQUENCE_EXTENT, HEADS * DV), DV ** -0.5, 0.25, ((0, 16),)),
        "log_forget": draw_log_forget(jax.random.fold_in(jax.random.fold_in(key_list[7], part), 71), part),
        "input_pre": jnp.clip(-3.0 + 3.5 * jax.random.uniform(part_splits[5], (SEQUENCE_EXTENT, HEADS), jnp.float32) ** block_scale(part_splits[5], (SEQUENCE_EXTENT, HEADS), ((0, 16),), -0.2, 0.2), -3.0, 0.5),
        "doc_starts": draw_doc_starts(jax.random.fold_in(jax.random.fold_in(key_list[7], part), 71), part),
    }


def rounded(values):
    return lax.optimization_barrier(values.astype(jnp.bfloat16)).astype(jnp.float32)


def mixing_ratio(form, left, right):
    return jnp.einsum(form, left.astype(jnp.float32), right.astype(jnp.float32), precision=lax.Precision.HIGHEST)


def gate_terms(log_gate, input_gate, start_flags):
    decay_sum = jnp.cumsum(log_gate, axis=0)
    segment = jnp.cumsum(start_flags.astype(jnp.int32), axis=0).astype(jnp.int32)
    final_seg = segment[-1]
    gate_logits = jnp.exp(input_gate)
    leading_weight = jnp.where((segment == 0)[:, None], jnp.exp(decay_sum), 0.0)
    trailing_weight = jnp.where((segment == final_seg)[:, None], jnp.exp(decay_sum[-1][None, :] - decay_sum), 0.0)
    carry_gain = jnp.where(final_seg == 0, jnp.exp(decay_sum[-1]), 0.0)
    return decay_sum, segment, gate_logits, leading_weight, trailing_weight, carry_gain


def reference(query_rows, key_rows, value_rows, out_grad, log_forget, input_pre, doc_starts):
    scale_factor = DK ** -0.5
    blocks = SEQUENCE_EXTENT // SPAN_POSITIONS
    query_all = query_rows.reshape(blocks, SPAN_POSITIONS, HEADS, DK)
    key_all = key_rows.reshape(blocks, SPAN_POSITIONS, HEADS, DK)
    value_all = value_rows.reshape(blocks, SPAN_POSITIONS, HEADS, DV)
    grad_all = out_grad.reshape(blocks, SPAN_POSITIONS, HEADS, DV)
    forget_all = log_forget.reshape(blocks, SPAN_POSITIONS, HEADS)
    input_all = input_pre.reshape(blocks, SPAN_POSITIONS, HEADS)
    start_all = doc_starts.reshape(blocks, SPAN_POSITIONS)
    inputs = (query_all, key_all, value_all, grad_all, forget_all, input_all, start_all)

    def prepare(items):
        query_block, key_block, value_block, gradient_block, forget_blk, input_blk, start_blk = items
        decay_sum, segment, gate_logits, leading_weight, trailing_weight, carry_gain = gate_terms(forget_blk, input_blk, start_blk)
        scaled_value = rounded((trailing_weight * gate_logits)[:, :, None] * value_block.astype(jnp.float32))
        ahead_carry_state = mixing_ratio("pxj,pxe->xje", key_block, scaled_value)
        scaled_query = rounded((scale_factor * leading_weight)[:, :, None] * query_block.astype(jnp.float32))
        reverse_carry_state = mixing_ratio("pxj,pxe->xje", scaled_query, gradient_block)
        return ahead_carry_state, reverse_carry_state, carry_gain

    forward_states, backward_states, gains = lax.map(prepare, inputs)

    def carry_step(carry, item):
        gain, state = item
        return gain[:, None, None] * carry + state, carry

    start_state = jnp.zeros((HEADS, DK, DV), jnp.float32)
    final_one, incoming = lax.scan(carry_step, start_state, (gains, forward_states))
    final_two, arriving = lax.scan(carry_step, start_state, (gains, backward_states), reverse=True)

    def finish(items):
        query_block, key_block, value_block, gradient_block, forget_blk, input_blk, start_blk, incoming_blk, arriving_blk = items
        decay_sum, segment, gate_logits, leading_weight, trailing_weight, carry_gain = gate_terms(forget_blk, input_blk, start_blk)
        position = jnp.arange(SPAN_POSITIONS)
        allowed = (position[:, None] >= position[None, :]) & (segment[:, None] == segment[None, :])
        gaps = decay_sum.T[:, :, None] - decay_sum.T[:, None, :]
        decay = jnp.exp(jnp.where(allowed[None], gaps, -jnp.inf))
        product = decay * mixing_ratio("thv,shv->hts", gradient_block, value_block)
        first_factor = rounded(scale_factor * product * gate_logits.T[:, None, :])
        second_factor = rounded(scale_factor * jnp.swapaxes(product, 1, 2))
        third_factor = rounded(scale_factor * jnp.swapaxes(decay, 1, 2) * mixing_ratio("thk,uhk->htu", key_block, query_block))
        incoming_state_block = rounded(incoming_blk)
        arriving_state_block = rounded(arriving_blk)
        query_gradient = mixing_ratio("row,wra->ora", first_factor, key_block) + scale_factor * leading_weight[:, :, None] * mixing_ratio("xrl,rml->xrm", gradient_block, incoming_state_block)
        key_gradient = gate_logits[:, :, None] * (mixing_ratio("bmz,zbo->mbo", second_factor, query_block) + trailing_weight[:, :, None] * mixing_ratio("xrl,rml->xrm", value_block, arriving_state_block))
        value_gradient = gate_logits[:, :, None] * (mixing_ratio("nyb,bnq->ynq", third_factor, gradient_block) + trailing_weight[:, :, None] * mixing_ratio("jam,ame->jae", key_block, arriving_state_block))
        return query_gradient.astype(jnp.bfloat16), key_gradient.astype(jnp.bfloat16), value_gradient.astype(jnp.bfloat16)

    query_gradient, key_gradient, value_gradient = lax.map(finish, inputs + (incoming, arriving))
    return (query_gradient.reshape(SEQUENCE_EXTENT, HEADS * DK), key_gradient.reshape(SEQUENCE_EXTENT, HEADS * DK), value_gradient.reshape(SEQUENCE_EXTENT, HEADS * DV))
```

```python
import functools

import jax
import jax.numpy as jnp
from jax import lax
from jax.experimental import pallas as pl
from jax.experimental.pallas import tpu as pltpu
from jax.sharding import PartitionSpec as P

F32 = jnp.float32
BF16 = jnp.bfloat16
LANES = 128
EXTRA = 8
DECAY, GATE, TAIL, HEAD, SEG, TAIL_GATE, GAIN, ROWS = 0, 4, 8, 12, 16, 24, 28, 32
VM = pl.BlockSpec(memory_space=pltpu.VMEM)
HBM = pl.BlockSpec(memory_space=pltpu.HBM)


def nt(a, b):
    return lax.dot_general(a, b, (((1,), (1,)), ((), ())), preferred_element_type=F32)


def nn(a, b):
    return lax.dot_general(a, b, (((1,), (0,)), ((), ())), preferred_element_type=F32)


def tn(a, b):
    return lax.dot_general(a, b, (((0,), (0,)), ((), ())), preferred_element_type=F32)


def three_terms(x):
    hi = x.astype(BF16)
    rest = x - hi.astype(F32)
    mid = rest.astype(BF16)
    lo = (rest - mid.astype(F32)).astype(BF16)
    return hi, mid, lo


def running_sums(x):
    rows, width = x.shape
    cuts = width // LANES
    stack = jnp.concatenate([x[:, i * LANES : (i + 1) * LANES] for i in range(cuts)], axis=0)
    parts = jnp.concatenate([t.astype(F32) for t in three_terms(stack)], axis=0).astype(BF16)
    earlier = lax.broadcasted_iota(jnp.int32, (LANES, LANES), 0)
    later = lax.broadcasted_iota(jnp.int32, (LANES, LANES), 1)
    upper = jnp.where(earlier <= later, 1.0, 0.0).astype(BF16)
    sums = nn(parts, upper)
    m = rows * cuts
    sums = sums[:m] + sums[m : 2 * m] + sums[2 * m :]
    pieces, base = [], jnp.zeros((rows, 1), F32)
    for i in range(cuts):
        piece = sums[i * rows : (i + 1) * rows]
        pieces.append(piece + base)
        base = base + piece[:, LANES - 1 :]
    return jnp.concatenate(pieces, axis=1)


def gain_rows(gain):
    heads = gain.shape[0]
    wide = jnp.concatenate([jnp.broadcast_to(gain[h : h + 1], (EXTRA, LANES)) for h in range(heads)], axis=1)
    hi, mid, lo = (t.astype(F32) for t in three_terms(wide))
    row = lax.broadcasted_iota(jnp.int32, wide.shape, 0)
    out = jnp.where(row == 0, hi, jnp.where(row == 1, mid, jnp.where(row == 2, lo, 0.0)))
    return out.astype(BF16)


def gain_of(ref, at, heads):
    block = ref[at : at + EXTRA, :].astype(F32)
    total = block[0:1] + block[1:2] + block[2:3]
    return jnp.concatenate([total[:, h * LANES : (h + 1) * LANES] for h in range(heads)], axis=0)


def wide_row(gain, h, width):
    return jnp.concatenate([gain[h : h + 1]] * (width // LANES), axis=1)


def states_kernel(
    heads, scale, lf, ip, starts, q_in, k_in, v_in, g_in, send, keep, cols, rows, q, k, v, g, seg_in, sems
):
    width = q.shape[0]
    dk, dv = q.shape[1] // heads, v.shape[1] // heads
    copies = []
    for h in range(heads):
        for i, (src, dst, w) in enumerate(((k_in, k, dk), (v_in, v, dv), (q_in, q, dk), (g_in, g, dv))):
            at = pl.ds(h * w, w)
            copies.append(pltpu.make_async_copy(src.at[:, at], dst.at[:, at], sems.at[h, i]))
            copies[-1].start()
    seg_in[...] = jnp.zeros_like(seg_in)
    seg_in[0:heads, :] = lf[...]
    seg_in[heads : heads + 1, :] = starts[...].astype(F32)
    sums = running_sums(seg_in[...])
    decay_sum, segment = sums[0:heads], sums[heads : heads + 1]
    last, final_seg = decay_sum[:, width - 1 :], segment[:, width - 1 :]
    gate = jnp.exp(ip[...])
    tail = jnp.where(segment == final_seg, jnp.exp(last - decay_sum), 0.0)
    head = jnp.where(segment == 0.0, scale * jnp.exp(decay_sum), 0.0)
    gain = jnp.where(final_seg == 0.0, jnp.exp(last), 0.0)
    rows[DECAY : DECAY + heads, :] = decay_sum
    rows[GATE : GATE + heads, :] = gate
    rows[TAIL : TAIL + heads, :] = tail
    rows[HEAD : HEAD + heads, :] = head
    rows[SEG : SEG + 8, :] = jnp.broadcast_to(segment, (8, width))
    rows[TAIL_GATE : TAIL_GATE + heads, :] = tail * gate
    rows[GAIN : GAIN + heads, :] = jnp.broadcast_to(gain, (heads, width))
    cols[...] = rows[...].T
    even = lax.rem(lax.axis_index("ctx"), 2) == 0
    for h in range(heads):
        for copy in copies[4 * h : 4 * h + 4]:
            copy.wait()
        kk, vv = slice(h * dk, (h + 1) * dk), slice(h * dv, (h + 1) * dv)
        scaled_v = (cols[:, TAIL_GATE + h : TAIL_GATE + h + 1] * v[:, vv].astype(F32)).astype(BF16)
        scaled_q = (cols[:, HEAD + h : HEAD + h + 1] * q[:, kk].astype(F32)).astype(BF16)
        forward = tn(k[:, kk], scaled_v)
        backward = tn(scaled_q, g[:, vv])
        send[kk, :] = jnp.where(even, forward, backward).astype(BF16)
        keep[kk, :] = jnp.where(even, backward, forward)
    send[heads * dk :, :] = gain_rows(jnp.broadcast_to(gain, (heads, LANES)))


def chip_kernel(heads, keep, near, rows, out):
    n = keep.shape[0]
    dk, width = n // heads, keep.shape[1]
    own = rows[GAIN : GAIN + heads, 0:LANES]
    for h in range(heads):
        at = slice(h * dk, (h + 1) * dk)
        out[at, :] = (keep[at, :] + wide_row(own, h, width) * near[at, :].astype(F32)).astype(BF16)
    out[n:, :] = gain_rows(own * gain_of(near, n, heads))


def far_kernel(heads, first, second, out):
    n, width = out.shape
    dk = n // heads
    gain = gain_of(first, n, heads)
    for h in range(heads):
        at = slice(h * dk, (h + 1) * dk)
        out[at, :] = (first[at, :].astype(F32) + wide_row(gain, h, width) * second[at, :].astype(F32)).astype(BF16)


def block_kernel(heads, scale, q, k, v, g, cols, rows, gq, gk, gv):
    width = q.shape[0]
    half = width // 2
    dk, dv = q.shape[1] // heads, v.shape[1] // heads
    t = lax.broadcasted_iota(jnp.int32, (half, half), 0)
    u = lax.broadcasted_iota(jnp.int32, (half, half), 1)
    causal = t >= u
    spans = [slice(i * half, (i + 1) * half) for i in range(2)]
    seg_c = [cols[s, SEG : SEG + 1] for s in spans]
    seg_r = [rows[SEG : SEG + 1, s] for s in spans]
    pairs = ((0, 0), (1, 0), (1, 1))
    allowed = [(seg_c[a] == seg_r[b]) & causal if a == b else seg_c[a] == seg_r[b] for a, b in pairs]
    for h in range(heads):
        kk, vv = slice(h * dk, (h + 1) * dk), slice(h * dv, (h + 1) * dv)
        total_q, total_k, total_v = [None] * 2, [None] * 2, [None] * 2

        def add(total, i, x):
            total[i] = x if total[i] is None else total[i] + x

        for (a, b), ok in zip(pairs, allowed, strict=True):
            ra, rb = spans[a], spans[b]
            gap = cols[ra, DECAY + h : DECAY + h + 1] - rows[DECAY + h : DECAY + h + 1, rb]
            decay = scale * jnp.exp(jnp.where(ok, gap, -jnp.inf))
            product = decay * nt(g[ra, vv], v[rb, vv])
            first = (product * rows[GATE + h : GATE + h + 1, rb]).astype(BF16)
            third = (decay * nt(q[ra, kk], k[rb, kk])).astype(BF16)
            add(total_q, a, nn(first, k[rb, kk]))
            add(total_k, b, tn(product.astype(BF16), q[ra, kk]))
            add(total_v, b, tn(third, g[ra, vv]))
        for i in range(2):
            gate = cols[spans[i], GATE + h : GATE + h + 1]
            gq[spans[i], kk] = total_q[i]
            gk[spans[i], kk] = gate * total_k[i]
            gv[spans[i], vv] = gate * total_v[i]


def tail_kernel(
    heads, near, far, other, k, v, g, cols, gq, gk, gv, out_q, out_k, out_v, buf_q, buf_k, buf_v, sems
):
    n, width = far.shape
    dk, dv = n // heads, width
    even = lax.rem(lax.axis_index("ctx"), 2) == 0
    gain = gain_of(near, n, heads)
    copies = []
    for h in range(heads):
        kk, vv = slice(h * dk, (h + 1) * dk), slice(h * dv, (h + 1) * dv)
        x = far[kk, :].astype(F32)
        y = near[kk, :].astype(F32) + wide_row(gain, h, width) * other[kk, :].astype(F32)
        incoming = jnp.where(even, x, y).astype(BF16)
        arriving = jnp.where(even, y, x).astype(BF16)
        tail = cols[:, TAIL_GATE + h : TAIL_GATE + h + 1]
        buf_q[:, kk] = (gq[:, kk] + cols[:, HEAD + h : HEAD + h + 1] * nt(g[:, vv], incoming)).astype(BF16)
        buf_k[:, kk] = (gk[:, kk] + tail * nt(v[:, vv], arriving)).astype(BF16)
        buf_v[:, vv] = (gv[:, vv] + tail * nn(k[:, kk], arriving)).astype(BF16)
        for i, (src, dst, at) in enumerate(((buf_q, out_q, kk), (buf_k, out_k, kk), (buf_v, out_v, vv))):
            copies.append(pltpu.make_async_copy(src.at[:, at], dst.at[:, at], sems.at[h, i]))
            copies[-1].start()
    for copy in copies:
        copy.wait()


def call(kernel, outs, ins, specs_in, specs_out, scratch=(), mib=24, flops=0, moved=0):
    return pl.pallas_call(
        kernel,
        out_shape=[jax.ShapeDtypeStruct(*o) for o in outs],
        in_specs=specs_in,
        out_specs=specs_out,
        scratch_shapes=list(scratch),
        compiler_params=pltpu.CompilerParams(vmem_limit_bytes=mib << 20),
        cost_estimate=pl.CostEstimate(flops=flops, bytes_accessed=moved, transcendentals=0),
    )(*ins)


def in_hbm(x):
    return pltpu.with_memory_space_constraint(x, pltpu.HBM)


def swap(x, route):
    return lax.ppermute(x, "ctx", route)


def routes(size):
    chips = size // 2
    both = lambda pairs: [p for a, b in pairs for p in ((a, b), (b, a))]
    on_chip = both([(2 * c, 2 * c + 1) for c in range(chips)])
    adjacent = both([(2 * c + 1, 2 * c + 2) for c in range(chips - 1)])
    second = both([(2 * c + 1, 2 * c + 4) for c in range(chips - 2)])
    return on_chip, adjacent, second


def body(query_rows, key_rows, value_rows, out_grad, log_forget, input_pre, doc_starts):
    width, heads = log_forget.shape
    dk, dv = query_rows.shape[1] // heads, value_rows.shape[1] // heads
    scale = dk ** (-0.5)
    n = heads * dk
    on_chip, adjacent, second = routes(lax.axis_size("ctx"))
    unit = 2 * width * dk * dv * heads
    send, keep, cols, rows, q, k, v, g = call(
        functools.partial(states_kernel, heads, scale),
        [
            ((n + EXTRA, dv), BF16),
            ((n, dv), F32),
            ((width, ROWS), F32),
            ((ROWS, width), F32),
            (query_rows.shape, BF16),
            (key_rows.shape, BF16),
            (value_rows.shape, BF16),
            (out_grad.shape, BF16),
        ],
        (log_forget.T, input_pre.T, doc_starts.reshape(1, width))
        + tuple(in_hbm(x) for x in (query_rows, key_rows, value_rows, out_grad)),
        [VM, VM, VM, HBM, HBM, HBM, HBM],
        [VM] * 8,
        [pltpu.VMEM((8, width), F32), pltpu.SemaphoreType.DMA((heads, 4))],
        flops=2 * unit,
        moved=12 << 20,
    )
    near = swap(send, on_chip)
    (chip,) = call(
        functools.partial(chip_kernel, heads), [((n + EXTRA, dv), BF16)], (keep, near, rows), [VM] * 3, [VM], mib=16
    )
    first = swap(chip, adjacent)
    later = swap(chip, second)
    gq, gk, gv = call(
        functools.partial(block_kernel, heads, scale),
        [((width, n), F32), ((width, n), F32), ((width, heads * dv), F32)],
        (q, k, v, g, cols, rows),
        [VM] * 6,
        [VM] * 3,
        flops=8 * unit,
        moved=14 << 20,
    )
    first, later, gq = lax.optimization_barrier((first, later, gq))
    (far,) = call(functools.partial(far_kernel, heads), [((n, dv), BF16)], (first, later), [VM] * 2, [VM], mib=16)
    other = swap(far, on_chip)
    return tuple(
        call(
            functools.partial(tail_kernel, heads),
            [(query_rows.shape, BF16), (key_rows.shape, BF16), (value_rows.shape, BF16)],
            (near, far, other, k, v, g, cols, gq, gk, gv),
            [VM] * 10,
            [HBM] * 3,
            [
                pltpu.VMEM(query_rows.shape, BF16),
                pltpu.VMEM(key_rows.shape, BF16),
                pltpu.VMEM(value_rows.shape, BF16),
                pltpu.SemaphoreType.DMA((heads, 3)),
            ],
            flops=3 * unit,
            moved=17 << 20,
        )
    )


def solution(mesh):
    row = P(("groups", "ctx"), None)
    in_specs = (row,) * 6 + (P(("groups", "ctx")),)
    return jax.shard_map(body, mesh=mesh, in_specs=in_specs, out_specs=(row,) * 3, check_vma=False)
```

```python
import functools

import jax
import jax.numpy as jnp
from jax import lax
from jax.experimental import pallas as pl
from jax.experimental.pallas import tpu as pltpu
from jax.sharding import PartitionSpec as P

F32 = jnp.float32
BF16 = jnp.bfloat16
LANES = 128
EXTRA = 8
CHUNKS = (2, 2)
DECAY, GATE, TAIL, HEAD, SEG, TAIL_GATE, GAIN, ROWS = 0, 4, 8, 12, 16, 24, 28, 32
VM = pl.BlockSpec(memory_space=pltpu.VMEM)
HBM = pl.BlockSpec(memory_space=pltpu.HBM)


def nt(a, b):
    return lax.dot_general(a, b, (((1,), (1,)), ((), ())), preferred_element_type=F32)


def nn(a, b):
    return lax.dot_general(a, b, (((1,), (0,)), ((), ())), preferred_element_type=F32)


def tn(a, b):
    return lax.dot_general(a, b, (((0,), (0,)), ((), ())), preferred_element_type=F32)


def three_terms(x):
    hi = x.astype(BF16)
    rest = x - hi.astype(F32)
    mid = rest.astype(BF16)
    lo = (rest - mid.astype(F32)).astype(BF16)
    return hi, mid, lo


def running_sums(x):
    rows, width = x.shape
    cuts = width // LANES
    stack = jnp.concatenate([x[:, i * LANES : (i + 1) * LANES] for i in range(cuts)], axis=0)
    parts = jnp.concatenate([t.astype(F32) for t in three_terms(stack)], axis=0).astype(BF16)
    earlier = lax.broadcasted_iota(jnp.int32, (LANES, LANES), 0)
    later = lax.broadcasted_iota(jnp.int32, (LANES, LANES), 1)
    upper = jnp.where(earlier <= later, 1.0, 0.0).astype(BF16)
    sums = nn(parts, upper)
    m = rows * cuts
    sums = sums[:m] + sums[m : 2 * m] + sums[2 * m :]
    pieces, base = [], jnp.zeros((rows, 1), F32)
    for i in range(cuts):
        piece = sums[i * rows : (i + 1) * rows]
        pieces.append(piece + base)
        base = base + piece[:, LANES - 1 :]
    return jnp.concatenate(pieces, axis=1)


def gain_rows(gain, width):
    wide = [jnp.broadcast_to(gain[i : i + 1], (EXTRA, LANES)) for i in range(gain.shape[0])]
    wide = jnp.concatenate(wide + [jnp.zeros((EXTRA, width - LANES * len(wide)), F32)], axis=1)
    hi, mid, lo = (t.astype(F32) for t in three_terms(wide))
    row = lax.broadcasted_iota(jnp.int32, wide.shape, 0)
    out = jnp.where(row == 0, hi, jnp.where(row == 1, mid, jnp.where(row == 2, lo, 0.0)))
    return out.astype(BF16)


def gain_of(ref, at, heads):
    block = ref[at : at + EXTRA, :].astype(F32)
    total = block[0:1] + block[1:2] + block[2:3]
    return jnp.concatenate([total[:, h * LANES : (h + 1) * LANES] for h in range(heads)], axis=0)


def wide_row(gain, h, width):
    return jnp.concatenate([gain[h : h + 1]] * (width // LANES), axis=1)


def states_of(span, heads, q, k, v, g, cols, rows, send, keep):
    dk, dv = q.shape[1] // heads, v.shape[1] // heads
    even = lax.rem(lax.axis_index("ctx"), 2) == 0
    for i, h in enumerate(span):
        kk, vv, at = slice(h * dk, (h + 1) * dk), slice(h * dv, (h + 1) * dv), slice(i * dk, (i + 1) * dk)
        scaled_v = (cols[:, TAIL_GATE + h : TAIL_GATE + h + 1] * v[:, vv].astype(F32)).astype(BF16)
        scaled_q = (cols[:, HEAD + h : HEAD + h + 1] * q[:, kk].astype(F32)).astype(BF16)
        forward = tn(k[:, kk], scaled_v)
        backward = tn(scaled_q, g[:, vv])
        send[at, :] = jnp.where(even, forward, backward).astype(BF16)
        keep[at, :] = jnp.where(even, backward, forward)
    send[len(span) * dk :, :] = gain_rows(rows[GAIN + span[0] : GAIN + span[-1] + 1, 0:LANES], dv)


def first_kernel(
    span, heads, scale, lf_in, ip_in, st_in, q_in, k_in, v_in, g_in, send, keep, cols, rows, q, k, v, g, lf, ip, st, sems, small
):
    width = q.shape[0]
    dk, dv = q.shape[1] // heads, v.shape[1] // heads
    gates = [pltpu.make_async_copy(x, y, small.at[i]) for i, (x, y) in enumerate(((lf_in, lf), (ip_in, ip), (st_in, st)))]
    for copy in gates:
        copy.start()
    copies = []
    for h in range(heads):
        for i, (src, dst, w) in enumerate(((k_in, k, dk), (v_in, v, dv), (q_in, q, dk), (g_in, g, dv))):
            at = pl.ds(h * w, w)
            copies.append(pltpu.make_async_copy(src.at[:, at], dst.at[:, at], sems.at[h, i]))
    now, after = copies[: 4 * len(span)], copies[4 * len(span) :]
    for copy in now:
        copy.start()
    for copy in gates:
        copy.wait()
    for copy in after:
        copy.start()
    filler = jnp.zeros((7 - heads, width), F32)
    sums = running_sums(jnp.concatenate([lf[...], st[...].astype(F32), filler], axis=0))
    decay_sum, segment = sums[0:heads], sums[heads : heads + 1]
    last, final_seg = decay_sum[:, width - 1 :], segment[:, width - 1 :]
    gate = jnp.exp(ip[...])
    tail = jnp.where(segment == final_seg, jnp.exp(last - decay_sum), 0.0)
    head = jnp.where(segment == 0.0, scale * jnp.exp(decay_sum), 0.0)
    gain = jnp.where(final_seg == 0.0, jnp.exp(last), 0.0)
    rows[DECAY : DECAY + heads, :] = decay_sum
    rows[GATE : GATE + heads, :] = gate
    rows[TAIL : TAIL + heads, :] = tail
    rows[HEAD : HEAD + heads, :] = head
    rows[SEG : SEG + 8, :] = jnp.broadcast_to(segment, (8, width))
    rows[TAIL_GATE : TAIL_GATE + heads, :] = tail * gate
    rows[GAIN : GAIN + heads, :] = jnp.broadcast_to(gain, (heads, width))
    cols[...] = rows[...].T
    for copy in now:
        copy.wait()
    states_of(span, heads, q, k, v, g, cols, rows, send, keep)
    for copy in after:
        copy.wait()


def next_kernel(span, heads, q, k, v, g, cols, rows, send, keep):
    states_of(span, heads, q, k, v, g, cols, rows, send, keep)


def chip_kernel(span, keep, near, rows, out, token):
    token[...] = jnp.zeros_like(token)
    n, width = keep.shape
    m = len(span)
    dk = n // m
    own = rows[GAIN + span[0] : GAIN + span[-1] + 1, 0:LANES]
    for i in range(m):
        at = slice(i * dk, (i + 1) * dk)
        out[at, :] = (keep[at, :] + wide_row(own, i, width) * near[at, :].astype(F32)).astype(BF16)
    out[n:, :] = gain_rows(own * gain_of(near, n, m), width)


def far_kernel(m, second, first, token, out):
    n, width = out.shape
    dk = n // m
    gain = gain_of(first, n, m)
    for i in range(m):
        at = slice(i * dk, (i + 1) * dk)
        out[at, :] = (first[at, :].astype(F32) + wide_row(gain, i, width) * second[at, :].astype(F32)).astype(BF16)


def block_kernel(heads, scale, q, k, v, g, cols, rows, ready, gq, gk, gv, token):
    token[...] = jnp.zeros_like(token)
    width = q.shape[0]
    half = width // 2
    dk, dv = q.shape[1] // heads, v.shape[1] // heads
    t = lax.broadcasted_iota(jnp.int32, (half, half), 0)
    u = lax.broadcasted_iota(jnp.int32, (half, half), 1)
    causal = t >= u
    spans = [slice(i * half, (i + 1) * half) for i in range(2)]
    seg_c = [cols[s, SEG : SEG + 1] for s in spans]
    seg_r = [rows[SEG : SEG + 1, s] for s in spans]
    pairs = ((0, 0), (1, 0), (1, 1))
    allowed = [(seg_c[a] == seg_r[b]) & causal if a == b else seg_c[a] == seg_r[b] for a, b in pairs]
    for h in range(heads):
        kk, vv = slice(h * dk, (h + 1) * dk), slice(h * dv, (h + 1) * dv)
        total_q, total_k, total_v = [None] * 2, [None] * 2, [None] * 2

        def add(total, i, x):
            total[i] = x if total[i] is None else total[i] + x

        for (a, b), ok in zip(pairs, allowed, strict=True):
            ra, rb = spans[a], spans[b]
            gap = cols[ra, DECAY + h : DECAY + h + 1] - rows[DECAY + h : DECAY + h + 1, rb]
            decay = scale * jnp.exp(jnp.where(ok, gap, -jnp.inf))
            product = decay * nt(g[ra, vv], v[rb, vv])
            first = (product * rows[GATE + h : GATE + h + 1, rb]).astype(BF16)
            third = (decay * nt(q[ra, kk], k[rb, kk])).astype(BF16)
            add(total_q, a, nn(first, k[rb, kk]))
            add(total_k, b, tn(product.astype(BF16), q[ra, kk]))
            add(total_v, b, tn(third, g[ra, vv]))
        for i in range(2):
            gate = cols[spans[i], GATE + h : GATE + h + 1]
            gq[spans[i], kk] = total_q[i]
            gk[spans[i], kk] = gate * total_k[i]
            gv[spans[i], vv] = gate * total_v[i]


def tail_kernel(span, heads, near, far, other, k, v, g, cols, gq, gk, gv, *refs):
    out_q, out_k, out_v, token, buf_q, buf_k, buf_v, sems = refs[-8:]
    token[...] = jnp.zeros_like(token)
    n, width = far.shape
    m = len(span)
    dk, dv = n // m, width
    even = lax.rem(lax.axis_index("ctx"), 2) == 0
    gain = gain_of(near, n, m)
    copies = []
    for i, h in enumerate(span):
        kk, vv, at = slice(h * dk, (h + 1) * dk), slice(h * dv, (h + 1) * dv), slice(i * dk, (i + 1) * dk)
        bv = slice(i * dv, (i + 1) * dv)
        x = far[at, :].astype(F32)
        y = near[at, :].astype(F32) + wide_row(gain, i, width) * other[at, :].astype(F32)
        incoming = jnp.where(even, x, y).astype(BF16)
        arriving = jnp.where(even, y, x).astype(BF16)
        tail = cols[:, TAIL_GATE + h : TAIL_GATE + h + 1]
        buf_q[:, at] = (gq[:, kk] + cols[:, HEAD + h : HEAD + h + 1] * nt(g[:, vv], incoming)).astype(BF16)
        buf_k[:, at] = (gk[:, kk] + tail * nt(v[:, vv], arriving)).astype(BF16)
        buf_v[:, bv] = (gv[:, vv] + tail * nn(k[:, kk], arriving)).astype(BF16)
        for j, (src, a, dst, b) in enumerate(((buf_q, at, out_q, kk), (buf_k, at, out_k, kk), (buf_v, bv, out_v, vv))):
            copies.append(pltpu.make_async_copy(src.at[:, a], dst.at[:, b], sems.at[i, j]))
            copies[-1].start()
    for copy in copies:
        copy.wait()


def call(kernel, outs, ins, specs_in, specs_out, scratch=(), mib=20, flops=0, moved=0, aliases=None):
    return pl.pallas_call(
        kernel,
        out_shape=[jax.ShapeDtypeStruct(*o) for o in outs],
        in_specs=specs_in,
        out_specs=specs_out,
        scratch_shapes=list(scratch),
        input_output_aliases=aliases or {},
        compiler_params=pltpu.CompilerParams(vmem_limit_bytes=mib << 20),
        cost_estimate=pl.CostEstimate(flops=flops // 1000000, bytes_accessed=moved // 1000000, transcendentals=0),
    )(*ins)


def in_hbm(x):
    return pltpu.with_memory_space_constraint(x, pltpu.HBM)


def swap(x, route):
    return lax.ppermute(x, "ctx", route)


def routes(size):
    chips = size // 2
    both = lambda pairs: [p for a, b in pairs for p in ((a, b), (b, a))]
    on_chip = both([(2 * c, 2 * c + 1) for c in range(chips)])
    adjacent = both([(2 * c + 1, 2 * c + 2) for c in range(chips - 1)])
    second = both([(2 * c + 1, 2 * c + 4) for c in range(chips - 2)])
    return on_chip, adjacent, second


def body(query_rows, key_rows, value_rows, out_grad, log_forget, input_pre, doc_starts):
    width, heads = log_forget.shape
    dk, dv = query_rows.shape[1] // heads, value_rows.shape[1] // heads
    scale = dk ** (-0.5)
    on_chip, adjacent, second = routes(lax.axis_size("ctx"))
    unit = 2 * width * dk * dv
    spans, at = [], 0
    for m in CHUNKS:
        spans.append(tuple(range(at, at + m)))
        at += m
    payload = [((m * dk + EXTRA, dv), BF16) for m in CHUNKS]
    total = [((m * dk, dv), F32) for m in CHUNKS]
    send, keep, cols, rows, q, k, v, g = call(
        functools.partial(first_kernel, spans[0], heads, scale),
        [
            payload[0],
            total[0],
            ((width, ROWS), F32),
            ((ROWS, width), F32),
            (query_rows.shape, BF16),
            (key_rows.shape, BF16),
            (value_rows.shape, BF16),
            (out_grad.shape, BF16),
        ],
        tuple(
            in_hbm(x)
            for x in (
                log_forget.T, input_pre.T, doc_starts.reshape(1, width), query_rows, key_rows, value_rows, out_grad
            )
        ),
        [HBM] * 7,
        [VM] * 8,
        [
            pltpu.VMEM((heads, width), F32),
            pltpu.VMEM((heads, width), F32),
            pltpu.VMEM((1, width), jnp.int32),
            pltpu.SemaphoreType.DMA((heads, 4)),
            pltpu.SemaphoreType.DMA((3,)),
        ],
        flops=2 * unit * CHUNKS[0],
        moved=12 << 20,
    )
    sends, keeps = [send], [keep]
    for i in range(1, len(CHUNKS)):
        send, keep = call(
            functools.partial(next_kernel, spans[i], heads),
            [payload[i], total[i]],
            (q, k, v, g, cols, rows),
            [VM] * 6,
            [VM] * 2,
            flops=2 * unit * CHUNKS[i],
            moved=4 << 20,
        )
        sends.append(send)
        keeps.append(keep)
    nears, firsts, seconds = [], [], []
    for i, span in enumerate(spans):
        near = swap(sends[i], on_chip)
        if i + 1 < len(spans):
            near, sends[i + 1] = lax.optimization_barrier((near, sends[i + 1]))
        chip, token = call(
            functools.partial(chip_kernel, span),
            [payload[i], ((8, LANES), F32)],
            (keeps[i], near, rows),
            [VM] * 3,
            [VM] * 2,
            mib=8,
        )
        seconds.append(swap(chip, second))
        firsts.append(swap(chip, adjacent))
        nears.append(near)
    gq, gk, gv, token = call(
        functools.partial(block_kernel, heads, scale),
        [((width, heads * dk), F32), ((width, heads * dk), F32), ((width, heads * dv), F32), ((8, LANES), F32)],
        (q, k, v, g, cols, rows, token),
        [VM] * 7,
        [VM] * 4,
        flops=8 * unit * heads,
        moved=14 << 20,
    )
    outs, token = (), token
    for i, span in enumerate(spans):
        m = len(span)
        (far,) = call(functools.partial(far_kernel, m), [((m * dk, dv), BF16)], (seconds[i], firsts[i], token), [VM] * 3, [VM], mib=8)
        other = swap(far, on_chip)
        *outs, token = call(
            functools.partial(tail_kernel, span, heads),
            [(query_rows.shape, BF16), (key_rows.shape, BF16), (value_rows.shape, BF16), ((8, LANES), F32)],
            (nears[i], far, other, k, v, g, cols, gq, gk, gv) + tuple(in_hbm(x) for x in outs),
            [VM] * 10 + [HBM] * len(outs),
            [HBM] * 3 + [VM],
            [
                pltpu.VMEM((width, m * dk), BF16),
                pltpu.VMEM((width, m * dk), BF16),
                pltpu.VMEM((width, m * dv), BF16),
                pltpu.SemaphoreType.DMA((m, 3)),
            ],
            flops=3 * unit * m,
            moved=(17 << 20) // len(spans),
            aliases={10 + j: j for j in range(len(outs))},
        )
    return tuple(outs)


def solution(mesh):
    row = P(("groups", "ctx"), None)
    in_specs = (row,) * 6 + (P(("groups", "ctx")),)
    return jax.shard_map(body, mesh=mesh, in_specs=in_specs, out_specs=(row,) * 3, check_vma=False)
```

```python
import functools

import jax
import jax.numpy as jnp
from jax import lax
from jax.experimental import pallas as pl
from jax.experimental.pallas import tpu as pltpu
from jax.sharding import PartitionSpec as P

F32 = jnp.float32
BF16 = jnp.bfloat16
LANES = 128
EXTRA = 8
CHUNKS = (2, 2)
DECAY, GATE, TAIL, HEAD, SEG, TAIL_GATE, GAIN, ROWS = 0, 4, 8, 12, 16, 24, 28, 32
VM = pl.BlockSpec(memory_space=pltpu.VMEM)
HBM = pl.BlockSpec(memory_space=pltpu.HBM)


def nt(a, b):
    return lax.dot_general(a, b, (((1,), (1,)), ((), ())), preferred_element_type=F32)


def nn(a, b):
    return lax.dot_general(a, b, (((1,), (0,)), ((), ())), preferred_element_type=F32)


def tn(a, b):
    return lax.dot_general(a, b, (((0,), (0,)), ((), ())), preferred_element_type=F32)


def three_terms(x):
    hi = x.astype(BF16)
    rest = x - hi.astype(F32)
    mid = rest.astype(BF16)
    lo = (rest - mid.astype(F32)).astype(BF16)
    return hi, mid, lo


def running_sums(x):
    rows, width = x.shape
    cuts = width // LANES
    stack = jnp.concatenate([x[:, i * LANES : (i + 1) * LANES] for i in range(cuts)], axis=0)
    parts = jnp.concatenate([t.astype(F32) for t in three_terms(stack)], axis=0).astype(BF16)
    earlier = lax.broadcasted_iota(jnp.int32, (LANES, LANES), 0)
    later = lax.broadcasted_iota(jnp.int32, (LANES, LANES), 1)
    upper = jnp.where(earlier <= later, 1.0, 0.0).astype(BF16)
    sums = nn(parts, upper)
    m = rows * cuts
    sums = sums[:m] + sums[m : 2 * m] + sums[2 * m :]
    pieces, base = [], jnp.zeros((rows, 1), F32)
    for i in range(cuts):
        piece = sums[i * rows : (i + 1) * rows]
        pieces.append(piece + base)
        base = base + piece[:, LANES - 1 :]
    return jnp.concatenate(pieces, axis=1)


def gain_rows(gain, width):
    wide = [jnp.broadcast_to(gain[i : i + 1], (EXTRA, LANES)) for i in range(gain.shape[0])]
    wide = jnp.concatenate(wide + [jnp.zeros((EXTRA, width - LANES * len(wide)), F32)], axis=1)
    hi, mid, lo = (t.astype(F32) for t in three_terms(wide))
    row = lax.broadcasted_iota(jnp.int32, wide.shape, 0)
    out = jnp.where(row == 0, hi, jnp.where(row == 1, mid, jnp.where(row == 2, lo, 0.0)))
    return out.astype(BF16)


def gain_of(ref, at, heads):
    block = ref[at : at + EXTRA, :].astype(F32)
    total = block[0:1] + block[1:2] + block[2:3]
    return jnp.concatenate([total[:, h * LANES : (h + 1) * LANES] for h in range(heads)], axis=0)


def wide_row(gain, h, width):
    return jnp.concatenate([gain[h : h + 1]] * (width // LANES), axis=1)


def states_of(span, heads, q, k, v, g, cols, rows, send, keep):
    dk, dv = q.shape[1] // heads, v.shape[1] // heads
    even = lax.rem(lax.axis_index("ctx"), 2) == 0
    for i, h in enumerate(span):
        kk, vv, at = slice(h * dk, (h + 1) * dk), slice(h * dv, (h + 1) * dv), slice(i * dk, (i + 1) * dk)
        scaled_v = (cols[:, TAIL_GATE + h : TAIL_GATE + h + 1] * v[:, vv].astype(F32)).astype(BF16)
        scaled_q = (cols[:, HEAD + h : HEAD + h + 1] * q[:, kk].astype(F32)).astype(BF16)
        forward = tn(k[:, kk], scaled_v)
        backward = tn(scaled_q, g[:, vv])
        send[at, :] = jnp.where(even, forward, backward).astype(BF16)
        keep[at, :] = jnp.where(even, backward, forward)
    send[len(span) * dk :, :] = gain_rows(rows[GAIN + span[0] : GAIN + span[-1] + 1, 0:LANES], dv)


def first_kernel(
    span, heads, scale, lf_in, ip_in, st_in, q_in, k_in, v_in, g_in, send, keep, cols, rows, q, k, v, g, lf, ip, st, sems, small
):
    width = q.shape[0]
    dk, dv = q.shape[1] // heads, v.shape[1] // heads
    gates = [pltpu.make_async_copy(x, y, small.at[i]) for i, (x, y) in enumerate(((lf_in, lf), (ip_in, ip), (st_in, st)))]
    for copy in gates:
        copy.start()
    copies = []
    for h in range(heads):
        for i, (src, dst, w) in enumerate(((k_in, k, dk), (v_in, v, dv), (q_in, q, dk), (g_in, g, dv))):
            at = pl.ds(h * w, w)
            copies.append(pltpu.make_async_copy(src.at[:, at], dst.at[:, at], sems.at[h, i]))
    now, after = copies[: 4 * len(span)], copies[4 * len(span) :]
    for copy in now:
        copy.start()
    for copy in gates:
        copy.wait()
    for copy in after:
        copy.start()
    filler = jnp.zeros((7 - heads, width), F32)
    sums = running_sums(jnp.concatenate([lf[...], st[...].astype(F32), filler], axis=0))
    decay_sum, segment = sums[0:heads], sums[heads : heads + 1]
    last, final_seg = decay_sum[:, width - 1 :], segment[:, width - 1 :]
    gate = jnp.exp(ip[...])
    tail = jnp.where(segment == final_seg, jnp.exp(last - decay_sum), 0.0)
    head = jnp.where(segment == 0.0, scale * jnp.exp(decay_sum), 0.0)
    gain = jnp.where(final_seg == 0.0, jnp.exp(last), 0.0)
    rows[DECAY : DECAY + heads, :] = decay_sum
    rows[GATE : GATE + heads, :] = gate
    rows[TAIL : TAIL + heads, :] = tail
    rows[HEAD : HEAD + heads, :] = head
    rows[SEG : SEG + 8, :] = jnp.broadcast_to(segment, (8, width))
    rows[TAIL_GATE : TAIL_GATE + heads, :] = tail * gate
    rows[GAIN : GAIN + heads, :] = jnp.broadcast_to(gain, (heads, width))
    cols[...] = rows[...].T
    for copy in now:
        copy.wait()
    states_of(span, heads, q, k, v, g, cols, rows, send, keep)
    for copy in after:
        copy.wait()


def next_kernel(span, heads, q, k, v, g, cols, rows, send, keep):
    states_of(span, heads, q, k, v, g, cols, rows, send, keep)


def chip_kernel(span, keep, near, rows, *refs):
    out, token = refs[-2:] if len(refs) == 2 else refs[1:3]
    token[...] = jnp.zeros_like(token)
    n, width = keep.shape
    m = len(span)
    dk = n // m
    own = rows[GAIN + span[0] : GAIN + span[-1] + 1, 0:LANES]
    for i in range(m):
        at = slice(i * dk, (i + 1) * dk)
        out[at, :] = (keep[at, :] + wide_row(own, i, width) * near[at, :].astype(F32)).astype(BF16)
    out[n:, :] = gain_rows(own * gain_of(near, n, m), width)


def far_kernel(m, first, second, token, out):
    n, width = out.shape
    dk = n // m
    gain = gain_of(first, n, m)
    for i in range(m):
        at = slice(i * dk, (i + 1) * dk)
        out[at, :] = (first[at, :].astype(F32) + wide_row(gain, i, width) * second[at, :].astype(F32)).astype(BF16)


def block_kernel(span, heads, scale, q, k, v, g, cols, rows, ready, gq, gk, gv, token):
    token[...] = jnp.zeros_like(token)
    width = q.shape[0]
    half = width // 2
    dk, dv = q.shape[1] // heads, v.shape[1] // heads
    t = lax.broadcasted_iota(jnp.int32, (half, half), 0)
    u = lax.broadcasted_iota(jnp.int32, (half, half), 1)
    causal = t >= u
    spans = [slice(i * half, (i + 1) * half) for i in range(2)]
    seg_c = [cols[s, SEG : SEG + 1] for s in spans]
    seg_r = [rows[SEG : SEG + 1, s] for s in spans]
    pairs = ((0, 0), (1, 0), (1, 1))
    allowed = [(seg_c[a] == seg_r[b]) & causal if a == b else seg_c[a] == seg_r[b] for a, b in pairs]
    for n, h in enumerate(span):
        kk, vv = slice(h * dk, (h + 1) * dk), slice(h * dv, (h + 1) * dv)
        total_q, total_k, total_v = [None] * 2, [None] * 2, [None] * 2

        def add(total, i, x):
            total[i] = x if total[i] is None else total[i] + x

        for (a, b), ok in zip(pairs, allowed, strict=True):
            ra, rb = spans[a], spans[b]
            gap = cols[ra, DECAY + h : DECAY + h + 1] - rows[DECAY + h : DECAY + h + 1, rb]
            decay = scale * jnp.exp(jnp.where(ok, gap, -jnp.inf))
            product = decay * nt(g[ra, vv], v[rb, vv])
            first = (product * rows[GATE + h : GATE + h + 1, rb]).astype(BF16)
            third = (decay * nt(q[ra, kk], k[rb, kk])).astype(BF16)
            add(total_q, a, nn(first, k[rb, kk]))
            add(total_k, b, tn(product.astype(BF16), q[ra, kk]))
            add(total_v, b, tn(third, g[ra, vv]))
        for i in range(2):
            gate = cols[spans[i], GATE + h : GATE + h + 1]
            gq[spans[i], n * dk : (n + 1) * dk] = total_q[i]
            gk[spans[i], n * dk : (n + 1) * dk] = gate * total_k[i]
            gv[spans[i], n * dv : (n + 1) * dv] = gate * total_v[i]


def far_tail_kernel(span, far, k, v, g, cols, gq, gk, gv, *refs):
    out_q, out_k, out_v, buf_q, buf_k, buf_v, sems = refs[-7:]
    even = lax.rem(lax.axis_index("ctx"), 2) == 0
    state = lambda at, width: far[at, :]
    tail_terms(span, even, state, k, v, g, cols, gq, gk, gv, out_q, out_k, out_v, buf_q, buf_k, buf_v, sems)


def near_tail_kernel(span, marks, near, other, far_ready, k, v, g, cols, gq, gk, gv, *refs):
    out_q, out_k, out_v = refs[-7 - marks : -4 - marks]
    buf_q, buf_k, buf_v, sems = refs[-4:]
    for token in refs[-4 - marks : -4]:
        token[...] = jnp.zeros_like(token)
    odd = lax.rem(lax.axis_index("ctx"), 2) == 1
    n, width = other.shape
    gain = gain_of(near, n, len(span))
    dk = n // len(span)

    def state(at, width):
        i = at.start // dk
        return (near[at, :].astype(F32) + wide_row(gain, i, width) * other[at, :].astype(F32)).astype(BF16)

    tail_terms(span, odd, state, k, v, g, cols, gq, gk, gv, out_q, out_k, out_v, buf_q, buf_k, buf_v, sems)


def tail_terms(span, incoming, state, k, v, g, cols, gq, gk, gv, out_q, out_k, out_v, buf_q, buf_k, buf_v, sems):
    m = len(span)
    dk, dv = gk.shape[1] // m, gv.shape[1] // m

    def copy_out(i, h, j):
        src, dst, w = ((buf_q, out_q, dk), (buf_k, out_k, dk), (buf_v, out_v, dv))[j]
        return pltpu.make_async_copy(
            src.at[:, i * w : (i + 1) * w], dst.at[:, h * w : (h + 1) * w], sems.at[i, j]
        )

    def spans_of(i, h):
        return (slice(i * dk, (i + 1) * dk), slice(h * dk, (h + 1) * dk)), (slice(i * dv, (i + 1) * dv), slice(h * dv, (h + 1) * dv))

    @pl.when(incoming)
    def _():
        copies = []
        for i, h in enumerate(span):
            (at, kk), (_, vv) = spans_of(i, h)
            head = cols[:, HEAD + h : HEAD + h + 1]
            buf_q[:, at] = (gq[:, at] + head * nt(g[:, vv], state(at, dv))).astype(BF16)
            copies.append(copy_out(i, h, 0))
            copies[-1].start()
        for copy in copies:
            copy.wait()

    @pl.when(jnp.logical_not(incoming))
    def _():
        copies = []
        for i, h in enumerate(span):
            (at, kk), (bv, vv) = spans_of(i, h)
            tail = cols[:, TAIL_GATE + h : TAIL_GATE + h + 1]
            arriving = state(at, dv)
            buf_v[:, bv] = (gv[:, bv] + tail * nn(k[:, kk], arriving)).astype(BF16)
            copies.append(copy_out(i, h, 2))
            copies[-1].start()
            buf_k[:, at] = (gk[:, at] + tail * nt(v[:, vv], arriving)).astype(BF16)
            copies.append(copy_out(i, h, 1))
            copies[-1].start()
        for copy in copies:
            copy.wait()


def call(kernel, outs, ins, specs_in, specs_out, scratch=(), mib=20, aliases=None):
    return pl.pallas_call(
        kernel,
        out_shape=[jax.ShapeDtypeStruct(*o) for o in outs],
        in_specs=specs_in,
        out_specs=specs_out,
        scratch_shapes=list(scratch),
        input_output_aliases=aliases or {},
        compiler_params=pltpu.CompilerParams(vmem_limit_bytes=mib << 20),
        cost_estimate=pl.CostEstimate(flops=1000, bytes_accessed=1000, transcendentals=0),
    )(*ins)


def in_hbm(x):
    return pltpu.with_memory_space_constraint(x, pltpu.HBM)


def swap(x, route):
    return lax.ppermute(x, "ctx", route)


def routes(size):
    chips = size // 2
    both = lambda pairs: [p for a, b in pairs for p in ((a, b), (b, a))]
    on_chip = both([(2 * c, 2 * c + 1) for c in range(chips)])
    adjacent = both([(2 * c + 1, 2 * c + 2) for c in range(chips - 1)])
    second = both([(2 * c + 1, 2 * c + 4) for c in range(chips - 2)])
    return on_chip, adjacent, second


def body(query_rows, key_rows, value_rows, out_grad, log_forget, input_pre, doc_starts):
    width, heads = log_forget.shape
    dk, dv = query_rows.shape[1] // heads, value_rows.shape[1] // heads
    scale = dk ** (-0.5)
    on_chip, adjacent, second = routes(lax.axis_size("ctx"))
    spans, at = [], 0
    for m in CHUNKS:
        spans.append(tuple(range(at, at + m)))
        at += m
    big = tuple(in_hbm(x) for x in (query_rows, key_rows, value_rows, out_grad))
    small = tuple(in_hbm(x) for x in (log_forget.T, input_pre.T, doc_starts.reshape(1, width)))
    mark = ((8, LANES), F32)
    payload = [((m * dk + EXTRA, dv), BF16) for m in CHUNKS]
    total = [((m * dk, dv), F32) for m in CHUNKS]
    send, keep, cols, rows, q, k, v, g = call(
        functools.partial(first_kernel, spans[0], heads, scale),
        [payload[0], total[0], ((width, ROWS), F32), ((ROWS, width), F32)] + [(x.shape, BF16) for x in big],
        small + big,
        [HBM] * 7,
        [VM] * 8,
        [
            pltpu.VMEM((heads, width), F32),
            pltpu.VMEM((heads, width), F32),
            pltpu.VMEM((1, width), jnp.int32),
            pltpu.SemaphoreType.DMA((heads, 4)),
            pltpu.SemaphoreType.DMA((3,)),
        ],
    )
    sends, keeps = [send], [keep]
    for i in range(1, len(CHUNKS)):
        send, keep = call(
            functools.partial(next_kernel, spans[i], heads),
            [payload[i], total[i]],
            (q, k, v, g, cols, rows),
            [VM] * 6,
            [VM] * 2,
        )
        sends.append(send)
        keeps.append(keep)
    nears, firsts, seconds = [], [], []
    for i, span in enumerate(spans):
        near = swap(sends[i], on_chip)
        chip, token, *later = call(
            functools.partial(chip_kernel, span),
            [payload[i], mark] + payload[i + 1 : i + 2],
            (keeps[i], near, rows, *sends[i + 1 : i + 2]),
            [VM] * (3 + len(sends[i + 1 : i + 2])),
            [VM] * (2 + len(sends[i + 1 : i + 2])),
            mib=8,
            aliases={3: 2} if i + 1 < len(spans) else None,
        )
        sends[i + 1 : i + 2] = later
        firsts.append(swap(chip, adjacent))
        seconds.append(swap(chip, second))
        nears.append(near)
    blocks = []
    for i, span in enumerate(spans):
        m = len(span)
        *block, token = call(
            functools.partial(block_kernel, span, heads, scale),
            [((width, m * dk), F32), ((width, m * dk), F32), ((width, m * dv), F32), mark],
            (q, k, v, g, cols, rows, token),
            [VM] * 7,
            [VM] * 4,
        )
        blocks.append(block)
    outs = ()
    shapes = [(query_rows.shape, BF16), (key_rows.shape, BF16), (value_rows.shape, BF16)]
    for i, span in enumerate(spans):
        m = len(span)
        (far,) = call(
            functools.partial(far_kernel, m),
            [((m * dk, dv), BF16)],
            (firsts[i], seconds[i], token),
            [VM] * 3,
            [VM],
            mib=8,
        )
        other = swap(far, on_chip)
        scratch = [
            pltpu.VMEM((width, m * dk), BF16),
            pltpu.VMEM((width, m * dk), BF16),
            pltpu.VMEM((width, m * dv), BF16),
            pltpu.SemaphoreType.DMA((m, 3)),
        ]
        outs = call(
            functools.partial(far_tail_kernel, span),
            shapes,
            (far, k, v, g, cols, *blocks[i]) + tuple(in_hbm(x) for x in outs),
            [VM] * 8 + [HBM] * len(outs),
            [HBM] * 3,
            scratch,
            aliases={8 + j: j for j in range(len(outs))},
        )
        marks = int(i + 1 < len(spans))
        outs = call(
            functools.partial(near_tail_kernel, span, marks),
            shapes + [mark] * marks,
            (nears[i], other, far, k, v, g, cols, *blocks[i]) + tuple(in_hbm(x) for x in outs),
            [VM] * 10 + [HBM] * len(outs),
            [HBM] * 3 + [VM] * marks,
            scratch,
            aliases={10 + j: j for j in range(len(outs))},
        )
        token, outs = outs[-1], outs[:3]
    return tuple(outs)


def solution(mesh):
    row = P(("groups", "ctx"), None)
    in_specs = (row,) * 6 + (P(("groups", "ctx")),)
    return jax.shard_map(body, mesh=mesh, in_specs=in_specs, out_specs=(row,) * 3, check_vma=False)
```

```python
import functools

import jax
import jax.numpy as jnp
from jax import lax
from jax.experimental import pallas as pl
from jax.experimental.pallas import tpu as pltpu
from jax.sharding import PartitionSpec as P

F32 = jnp.float32
BF16 = jnp.bfloat16
LANES = 128
EXTRA = 8
CHUNKS = (2, 2)
DECAY, GATE, TAIL, HEAD, SEG, TAIL_GATE, GAIN, ROWS = 0, 4, 8, 12, 16, 24, 28, 32
VM = pl.BlockSpec(memory_space=pltpu.VMEM)
HBM = pl.BlockSpec(memory_space=pltpu.HBM)


def nt(a, b):
    return lax.dot_general(a, b, (((1,), (1,)), ((), ())), preferred_element_type=F32)


def nn(a, b):
    return lax.dot_general(a, b, (((1,), (0,)), ((), ())), preferred_element_type=F32)


def tn(a, b):
    return lax.dot_general(a, b, (((0,), (0,)), ((), ())), preferred_element_type=F32)


def three_terms(x):
    hi = x.astype(BF16)
    rest = x - hi.astype(F32)
    mid = rest.astype(BF16)
    lo = (rest - mid.astype(F32)).astype(BF16)
    return hi, mid, lo


def running_sums(x):
    rows, width = x.shape
    cuts = width // LANES
    stack = jnp.concatenate([x[:, i * LANES : (i + 1) * LANES] for i in range(cuts)], axis=0)
    parts = jnp.concatenate([t.astype(F32) for t in three_terms(stack)], axis=0).astype(BF16)
    earlier = lax.broadcasted_iota(jnp.int32, (LANES, LANES), 0)
    later = lax.broadcasted_iota(jnp.int32, (LANES, LANES), 1)
    upper = jnp.where(earlier <= later, 1.0, 0.0).astype(BF16)
    sums = nn(parts, upper)
    m = rows * cuts
    sums = sums[:m] + sums[m : 2 * m] + sums[2 * m :]
    pieces, base = [], jnp.zeros((rows, 1), F32)
    for i in range(cuts):
        piece = sums[i * rows : (i + 1) * rows]
        pieces.append(piece + base)
        base = base + piece[:, LANES - 1 :]
    return jnp.concatenate(pieces, axis=1)


def gain_rows(gain, width):
    wide = [jnp.broadcast_to(gain[i : i + 1], (EXTRA, LANES)) for i in range(gain.shape[0])]
    wide = jnp.concatenate(wide + [jnp.zeros((EXTRA, width - LANES * len(wide)), F32)], axis=1)
    hi, mid, lo = (t.astype(F32) for t in three_terms(wide))
    row = lax.broadcasted_iota(jnp.int32, wide.shape, 0)
    out = jnp.where(row == 0, hi, jnp.where(row == 1, mid, jnp.where(row == 2, lo, 0.0)))
    return out.astype(BF16)


def gain_of(ref, at, heads):
    block = ref[at : at + EXTRA, :].astype(F32)
    total = block[0:1] + block[1:2] + block[2:3]
    return jnp.concatenate([total[:, h * LANES : (h + 1) * LANES] for h in range(heads)], axis=0)


def wide_row(gain, h, width):
    return jnp.concatenate([gain[h : h + 1]] * (width // LANES), axis=1)


def states_of(span, heads, q, k, v, g, cols, rows, send, keep):
    dk, dv = q.shape[1] // heads, v.shape[1] // heads
    even = lax.rem(lax.axis_index("ctx"), 2) == 0
    for i, h in enumerate(span):
        kk, vv, at = slice(h * dk, (h + 1) * dk), slice(h * dv, (h + 1) * dv), slice(i * dk, (i + 1) * dk)
        scaled_v = (cols[:, TAIL_GATE + h : TAIL_GATE + h + 1] * v[:, vv].astype(F32)).astype(BF16)
        scaled_q = (cols[:, HEAD + h : HEAD + h + 1] * q[:, kk].astype(F32)).astype(BF16)
        forward = tn(k[:, kk], scaled_v)
        backward = tn(scaled_q, g[:, vv])
        send[at, :] = jnp.where(even, forward, backward).astype(BF16)
        keep[at, :] = jnp.where(even, backward, forward)
    send[len(span) * dk :, :] = gain_rows(rows[GAIN + span[0] : GAIN + span[-1] + 1, 0:LANES], dv)


def first_kernel(
    span, heads, scale, lf_in, ip_in, st_in, q_in, k_in, v_in, g_in, send, keep, cols, rows, q, k, v, g, lf, ip, st, sems, small
):
    width = q.shape[0]
    dk, dv = q.shape[1] // heads, v.shape[1] // heads
    gates = [pltpu.make_async_copy(x, y, small.at[i]) for i, (x, y) in enumerate(((lf_in, lf), (ip_in, ip), (st_in, st)))]
    for copy in gates:
        copy.start()
    copies = []
    for h in range(heads):
        for i, (src, dst, w) in enumerate(((k_in, k, dk), (v_in, v, dv), (q_in, q, dk), (g_in, g, dv))):
            at = pl.ds(h * w, w)
            copies.append(pltpu.make_async_copy(src.at[:, at], dst.at[:, at], sems.at[h, i]))
    now, after = copies[: 4 * len(span)], copies[4 * len(span) :]
    for copy in now:
        copy.start()
    for copy in gates:
        copy.wait()
    for copy in after:
        copy.start()
    filler = jnp.zeros((7 - heads, width), F32)
    sums = running_sums(jnp.concatenate([lf[...], st[...].astype(F32), filler], axis=0))
    decay_sum, segment = sums[0:heads], sums[heads : heads + 1]
    last, final_seg = decay_sum[:, width - 1 :], segment[:, width - 1 :]
    gate = jnp.exp(ip[...])
    tail = jnp.where(segment == final_seg, jnp.exp(last - decay_sum), 0.0)
    head = jnp.where(segment == 0.0, scale * jnp.exp(decay_sum), 0.0)
    gain = jnp.where(final_seg == 0.0, jnp.exp(last), 0.0)
    rows[DECAY : DECAY + heads, :] = decay_sum
    rows[GATE : GATE + heads, :] = gate
    rows[TAIL : TAIL + heads, :] = tail
    rows[HEAD : HEAD + heads, :] = head
    rows[SEG : SEG + 8, :] = jnp.broadcast_to(segment, (8, width))
    rows[TAIL_GATE : TAIL_GATE + heads, :] = tail * gate
    rows[GAIN : GAIN + heads, :] = jnp.broadcast_to(gain, (heads, width))
    cols[...] = rows[...].T
    for copy in now:
        copy.wait()
    states_of(span, heads, q, k, v, g, cols, rows, send, keep)
    for copy in after:
        copy.wait()


def next_kernel(span, heads, q, k, v, g, cols, rows, send, keep):
    states_of(span, heads, q, k, v, g, cols, rows, send, keep)


def chip_kernel(span, keep, near, rows, *refs):
    through = (len(refs) - 3) // 2
    out, again, token = refs[through : through + 3]
    token[...] = jnp.zeros_like(token)
    n, width = keep.shape
    m = len(span)
    dk = n // m
    own = rows[GAIN + span[0] : GAIN + span[-1] + 1, 0:LANES]
    for i in range(m):
        at = slice(i * dk, (i + 1) * dk)
        out[at, :] = (keep[at, :] + wide_row(own, i, width) * near[at, :].astype(F32)).astype(BF16)
    out[n:, :] = gain_rows(own * gain_of(near, n, m), width)
    again[...] = out[...]


def through_kernel(after, x, token, out):
    del after, x, token, out


def far_kernel(m, second, first, relayed, token, out):
    n, width = out.shape
    dk = n // m
    gain = gain_of(first, n, m) + gain_of(relayed, n, m)
    for i in range(m):
        at = slice(i * dk, (i + 1) * dk)
        adjacent = first[at, :].astype(F32) + relayed[at, :].astype(F32)
        out[at, :] = (adjacent + wide_row(gain, i, width) * second[at, :].astype(F32)).astype(BF16)


def block_kernel(span, heads, scale, q, k, v, g, cols, rows, ready, *refs):
    gq, gk, gv, token = refs[:4] if len(refs) == 4 else refs[1:5]
    token[...] = jnp.zeros_like(token)
    width = q.shape[0]
    half = width // 2
    dk, dv = q.shape[1] // heads, v.shape[1] // heads
    t = lax.broadcasted_iota(jnp.int32, (half, half), 0)
    u = lax.broadcasted_iota(jnp.int32, (half, half), 1)
    causal = t >= u
    spans = [slice(i * half, (i + 1) * half) for i in range(2)]
    seg_c = [cols[s, SEG : SEG + 1] for s in spans]
    seg_r = [rows[SEG : SEG + 1, s] for s in spans]
    pairs = ((0, 0), (1, 0), (1, 1))
    allowed = [(seg_c[a] == seg_r[b]) & causal if a == b else seg_c[a] == seg_r[b] for a, b in pairs]
    for n, h in enumerate(span):
        kk, vv = slice(h * dk, (h + 1) * dk), slice(h * dv, (h + 1) * dv)
        total_q, total_k, total_v = [None] * 2, [None] * 2, [None] * 2

        def add(total, i, x):
            total[i] = x if total[i] is None else total[i] + x

        for (a, b), ok in zip(pairs, allowed, strict=True):
            ra, rb = spans[a], spans[b]
            gap = cols[ra, DECAY + h : DECAY + h + 1] - rows[DECAY + h : DECAY + h + 1, rb]
            decay = scale * jnp.exp(jnp.where(ok, gap, -jnp.inf))
            product = decay * nt(g[ra, vv], v[rb, vv])
            first = (product * rows[GATE + h : GATE + h + 1, rb]).astype(BF16)
            third = (decay * nt(q[ra, kk], k[rb, kk])).astype(BF16)
            add(total_q, a, nn(first, k[rb, kk]))
            add(total_k, b, tn(product.astype(BF16), q[ra, kk]))
            add(total_v, b, tn(third, g[ra, vv]))
        for i in range(2):
            gate = cols[spans[i], GATE + h : GATE + h + 1]
            gq[spans[i], n * dk : (n + 1) * dk] = total_q[i]
            gk[spans[i], n * dk : (n + 1) * dk] = gate * total_k[i]
            gv[spans[i], n * dv : (n + 1) * dv] = gate * total_v[i]


def far_tail_kernel(span, far, k, v, g, cols, gq, gk, gv, *refs):
    out_q, out_k, out_v, buf_q, buf_k, buf_v, sems = refs[-7:]
    even = lax.rem(lax.axis_index("ctx"), 2) == 0
    state = lambda at, width: far[at, :]
    tail_terms(span, even, state, k, v, g, cols, gq, gk, gv, out_q, out_k, out_v, buf_q, buf_k, buf_v, sems)


def near_tail_kernel(span, marks, near, other, far_ready, k, v, g, cols, gq, gk, gv, *refs):
    out_q, out_k, out_v = refs[-7 - marks : -4 - marks]
    buf_q, buf_k, buf_v, sems = refs[-4:]
    for token in refs[-4 - marks : -4]:
        token[...] = jnp.zeros_like(token)
    odd = lax.rem(lax.axis_index("ctx"), 2) == 1
    n, width = other.shape
    gain = gain_of(near, n, len(span))
    dk = n // len(span)

    def state(at, width):
        i = at.start // dk
        return (near[at, :].astype(F32) + wide_row(gain, i, width) * other[at, :].astype(F32)).astype(BF16)

    tail_terms(span, odd, state, k, v, g, cols, gq, gk, gv, out_q, out_k, out_v, buf_q, buf_k, buf_v, sems)


def tail_terms(span, incoming, state, k, v, g, cols, gq, gk, gv, out_q, out_k, out_v, buf_q, buf_k, buf_v, sems):
    m = len(span)
    dk, dv = gk.shape[1] // m, gv.shape[1] // m

    def copy_out(i, h, j):
        src, dst, w = ((buf_q, out_q, dk), (buf_k, out_k, dk), (buf_v, out_v, dv))[j]
        return pltpu.make_async_copy(
            src.at[:, i * w : (i + 1) * w], dst.at[:, h * w : (h + 1) * w], sems.at[i, j]
        )

    def spans_of(i, h):
        return (slice(i * dk, (i + 1) * dk), slice(h * dk, (h + 1) * dk)), (slice(i * dv, (i + 1) * dv), slice(h * dv, (h + 1) * dv))

    @pl.when(incoming)
    def _():
        copies = []
        for i, h in enumerate(span):
            (at, kk), (_, vv) = spans_of(i, h)
            head = cols[:, HEAD + h : HEAD + h + 1]
            buf_q[:, at] = (gq[:, at] + head * nt(g[:, vv], state(at, dv))).astype(BF16)
            copies.append(copy_out(i, h, 0))
            copies[-1].start()
        for copy in copies:
            copy.wait()

    @pl.when(jnp.logical_not(incoming))
    def _():
        copies = []
        for i, h in enumerate(span):
            (at, kk), (bv, vv) = spans_of(i, h)
            tail = cols[:, TAIL_GATE + h : TAIL_GATE + h + 1]
            arriving = state(at, dv)
            buf_v[:, bv] = (gv[:, bv] + tail * nn(k[:, kk], arriving)).astype(BF16)
            copies.append(copy_out(i, h, 2))
            copies[-1].start()
            buf_k[:, at] = (gk[:, at] + tail * nt(v[:, vv], arriving)).astype(BF16)
            copies.append(copy_out(i, h, 1))
            copies[-1].start()
        for copy in copies:
            copy.wait()


def call(kernel, outs, ins, specs_in, specs_out, scratch=(), mib=20, aliases=None):
    return pl.pallas_call(
        kernel,
        out_shape=[jax.ShapeDtypeStruct(*o) for o in outs],
        in_specs=specs_in,
        out_specs=specs_out,
        scratch_shapes=list(scratch),
        input_output_aliases=aliases or {},
        compiler_params=pltpu.CompilerParams(vmem_limit_bytes=mib << 20),
        cost_estimate=pl.CostEstimate(flops=1000, bytes_accessed=1000, transcendentals=0),
    )(*ins)


def in_hbm(x):
    return pltpu.with_memory_space_constraint(x, pltpu.HBM)


def swap(x, route):
    return lax.ppermute(x, "ctx", route)


def routes(size):
    chips = size // 2
    both = lambda pairs: [p for a, b in pairs for p in ((a, b), (b, a))]
    on_chip = both([(2 * c, 2 * c + 1) for c in range(chips)])
    mates = both([(2 * c + 1, 2 * c + 2) for c in range(0, chips, 2)])
    second = both([(2 * c + 1, 2 * c + 4) for c in range(chips - 2)])
    relay = [p for c in range(0, chips, 2) for p in ((2 * c + 2, 2 * c), (2 * c + 1, 2 * c + 3))]
    return on_chip, mates, second, relay


def body(query_rows, key_rows, value_rows, out_grad, log_forget, input_pre, doc_starts):
    width, heads = log_forget.shape
    dk, dv = query_rows.shape[1] // heads, value_rows.shape[1] // heads
    scale = dk ** (-0.5)
    on_chip, mates, second, relay = routes(lax.axis_size("ctx"))
    spans, at = [], 0
    for m in CHUNKS:
        spans.append(tuple(range(at, at + m)))
        at += m
    big = tuple(in_hbm(x) for x in (query_rows, key_rows, value_rows, out_grad))
    small = tuple(in_hbm(x) for x in (log_forget.T, input_pre.T, doc_starts.reshape(1, width)))
    mark = ((8, LANES), F32)
    payload = [((m * dk + EXTRA, dv), BF16) for m in CHUNKS]
    total = [((m * dk, dv), F32) for m in CHUNKS]
    send, keep, cols, rows, q, k, v, g = call(
        functools.partial(first_kernel, spans[0], heads, scale),
        [payload[0], total[0], ((width, ROWS), F32), ((ROWS, width), F32)] + [(x.shape, BF16) for x in big],
        small + big,
        [HBM] * 7,
        [VM] * 8,
        [
            pltpu.VMEM((heads, width), F32),
            pltpu.VMEM((heads, width), F32),
            pltpu.VMEM((1, width), jnp.int32),
            pltpu.SemaphoreType.DMA((heads, 4)),
            pltpu.SemaphoreType.DMA((3,)),
        ],
    )
    sends, keeps = [send], [keep]
    for i in range(1, len(CHUNKS)):
        send, keep = call(
            functools.partial(next_kernel, spans[i], heads),
            [payload[i], total[i]],
            (q, k, v, g, cols, rows),
            [VM] * 6,
            [VM] * 2,
        )
        sends.append(send)
        keeps.append(keep)
    nears, firsts, seconds, blocks, relayed = [], [], [], [], []
    passed = ()
    for i, span in enumerate(spans):
        near = swap(sends[i], on_chip)
        passed = passed + tuple(sends[i + 1 : i + 2])
        count = len(passed)
        chip, copy, token, *passed = call(
            functools.partial(chip_kernel, span),
            [payload[i]] * 2 + [mark] + [(x.shape, BF16) for x in passed],
            (keeps[i], near, rows, *passed),
            [VM] * (3 + count),
            [VM] * (3 + count),
            mib=8,
            aliases={3 + j: 3 + j for j in range(count)},
        )
        if i > 0:
            seconds.append(swap(passed[0], second))
        if i + 1 < len(spans):
            sends[i + 1] = passed[-1]
        passed = (copy,)
        firsts.append(swap(chip, mates))
        nears.append(near)
    seconds.append(swap(copy, second))
    passed = ()
    for i, span in enumerate(spans):
        m = len(span)
        count = len(passed)
        *block, token, = call(
            functools.partial(block_kernel, span, heads, scale),
            [((width, m * dk), F32), ((width, m * dk), F32), ((width, m * dv), F32), mark]
            + [(x.shape, BF16) for x in passed],
            (q, k, v, g, cols, rows, token, *passed),
            [VM] * (7 + count),
            [VM] * (4 + count),
            aliases={7 + j: 4 + j for j in range(count)},
        )
        if count:
            seconds.append(swap(token, second))
            *block, token = block
            passed = ()
        blocks.append(block)
        (seconds[i],) = call(
            through_kernel, payload[i : i + 1], (firsts[i], seconds[i], token), [VM] * 3, [VM], mib=8, aliases={1: 0}
        )
        relayed.append(swap(seconds[i], relay))
    outs = ()
    shapes = [(query_rows.shape, BF16), (key_rows.shape, BF16), (value_rows.shape, BF16)]
    for i, span in enumerate(spans):
        m = len(span)
        (far,) = call(
            functools.partial(far_kernel, m),
            [((m * dk, dv), BF16)],
            (seconds[i], firsts[i], relayed[i], token),
            [VM] * 4,
            [VM],
            mib=8,
        )
        other = swap(far, on_chip)
        scratch = [
            pltpu.VMEM((width, m * dk), BF16),
            pltpu.VMEM((width, m * dk), BF16),
            pltpu.VMEM((width, m * dv), BF16),
            pltpu.SemaphoreType.DMA((m, 3)),
        ]
        outs = call(
            functools.partial(far_tail_kernel, span),
            shapes,
            (far, k, v, g, cols, *blocks[i]) + tuple(in_hbm(x) for x in outs),
            [VM] * 8 + [HBM] * len(outs),
            [HBM] * 3,
            scratch,
            aliases={8 + j: j for j in range(len(outs))},
        )
        marks = int(i + 1 < len(spans))
        outs = call(
            functools.partial(near_tail_kernel, span, marks),
            shapes + [mark] * marks,
            (nears[i], other, far, k, v, g, cols, *blocks[i]) + tuple(in_hbm(x) for x in outs),
            [VM] * 10 + [HBM] * len(outs),
            [HBM] * 3 + [VM] * marks,
            scratch,
            aliases={10 + j: j for j in range(len(outs))},
        )
        token, outs = outs[-1], outs[:3]
    return tuple(outs)


def solution(mesh):
    row = P(("groups", "ctx"), None)
    in_specs = (row,) * 6 + (P(("groups", "ctx")),)
    return jax.shard_map(body, mesh=mesh, in_specs=in_specs, out_specs=(row,) * 3, check_vma=False)
```

```python
import functools

import jax
import jax.numpy as jnp
from jax import lax
from jax.experimental import pallas as pl
from jax.experimental.pallas import tpu as pltpu
from jax.sharding import PartitionSpec as P

F32 = jnp.float32
BF16 = jnp.bfloat16
LANES = 128
EXTRA = 8
CHUNKS = (2, 2)
DECAY, GATE, TAIL, HEAD, SEG, TAIL_GATE, GAIN, ROWS = 0, 4, 8, 12, 16, 24, 28, 32
VM = pl.BlockSpec(memory_space=pltpu.VMEM)
HBM = pl.BlockSpec(memory_space=pltpu.HBM)


def nt(a, b):
    return lax.dot_general(a, b, (((1,), (1,)), ((), ())), preferred_element_type=F32)


def nn(a, b):
    return lax.dot_general(a, b, (((1,), (0,)), ((), ())), preferred_element_type=F32)


def tn(a, b):
    return lax.dot_general(a, b, (((0,), (0,)), ((), ())), preferred_element_type=F32)


def three_terms(x):
    hi = x.astype(BF16)
    rest = x - hi.astype(F32)
    mid = rest.astype(BF16)
    lo = (rest - mid.astype(F32)).astype(BF16)
    return hi, mid, lo


def running_sums(x):
    rows, width = x.shape
    cuts = width // LANES
    stack = jnp.concatenate([x[:, i * LANES : (i + 1) * LANES] for i in range(cuts)], axis=0)
    parts = jnp.concatenate([t.astype(F32) for t in three_terms(stack)], axis=0).astype(BF16)
    earlier = lax.broadcasted_iota(jnp.int32, (LANES, LANES), 0)
    later = lax.broadcasted_iota(jnp.int32, (LANES, LANES), 1)
    upper = jnp.where(earlier <= later, 1.0, 0.0).astype(BF16)
    sums = nn(parts, upper)
    m = rows * cuts
    sums = sums[:m] + sums[m : 2 * m] + sums[2 * m :]
    pieces, base = [], jnp.zeros((rows, 1), F32)
    for i in range(cuts):
        piece = sums[i * rows : (i + 1) * rows]
        pieces.append(piece + base)
        base = base + piece[:, LANES - 1 :]
    return jnp.concatenate(pieces, axis=1)


def gain_rows(gain, width):
    wide = [jnp.broadcast_to(gain[i : i + 1], (EXTRA, LANES)) for i in range(gain.shape[0])]
    wide = jnp.concatenate(wide + [jnp.zeros((EXTRA, width - LANES * len(wide)), F32)], axis=1)
    hi, mid, lo = (t.astype(F32) for t in three_terms(wide))
    row = lax.broadcasted_iota(jnp.int32, wide.shape, 0)
    out = jnp.where(row == 0, hi, jnp.where(row == 1, mid, jnp.where(row == 2, lo, 0.0)))
    return out.astype(BF16)


def gain_of(ref, at, heads):
    block = ref[at : at + EXTRA, :].astype(F32)
    total = block[0:1] + block[1:2] + block[2:3]
    return jnp.concatenate([total[:, h * LANES : (h + 1) * LANES] for h in range(heads)], axis=0)


def wide_row(gain, h, width):
    return jnp.concatenate([gain[h : h + 1]] * (width // LANES), axis=1)


def states_of(span, heads, q, k, v, g, cols, rows, send, keep):
    dk, dv = q.shape[1] // heads, v.shape[1] // heads
    even = lax.rem(lax.axis_index("ctx"), 2) == 0
    for i, h in enumerate(span):
        kk, vv, at = slice(h * dk, (h + 1) * dk), slice(h * dv, (h + 1) * dv), slice(i * dk, (i + 1) * dk)
        scaled_v = (cols[:, TAIL_GATE + h : TAIL_GATE + h + 1] * v[:, vv].astype(F32)).astype(BF16)
        scaled_q = (cols[:, HEAD + h : HEAD + h + 1] * q[:, kk].astype(F32)).astype(BF16)
        forward = tn(k[:, kk], scaled_v)
        backward = tn(scaled_q, g[:, vv])
        send[at, :] = jnp.where(even, forward, backward).astype(BF16)
        keep[at, :] = jnp.where(even, backward, forward)
    send[len(span) * dk :, :] = gain_rows(rows[GAIN + span[0] : GAIN + span[-1] + 1, 0:LANES], dv)


def first_kernel(
    span, heads, scale, lf_in, ip_in, st_in, q_in, k_in, v_in, g_in, send, keep, cols, rows, q, k, v, g, lf, ip, st, sems, small
):
    width = q.shape[0]
    dk, dv = q.shape[1] // heads, v.shape[1] // heads
    gates = [pltpu.make_async_copy(x, y, small.at[i]) for i, (x, y) in enumerate(((lf_in, lf), (ip_in, ip), (st_in, st)))]
    for copy in gates:
        copy.start()
    copies = []
    for h in range(heads):
        for i, (src, dst, w) in enumerate(((k_in, k, dk), (v_in, v, dv), (q_in, q, dk), (g_in, g, dv))):
            at = pl.ds(h * w, w)
            copies.append(pltpu.make_async_copy(src.at[:, at], dst.at[:, at], sems.at[h, i]))
    now, after = copies[: 4 * len(span)], copies[4 * len(span) :]
    for copy in now:
        copy.start()
    for copy in gates:
        copy.wait()
    for copy in after:
        copy.start()
    filler = jnp.zeros((7 - heads, width), F32)
    sums = running_sums(jnp.concatenate([lf[...], st[...].astype(F32), filler], axis=0))
    decay_sum, segment = sums[0:heads], sums[heads : heads + 1]
    last, final_seg = decay_sum[:, width - 1 :], segment[:, width - 1 :]
    gate = jnp.exp(ip[...])
    tail = jnp.where(segment == final_seg, jnp.exp(last - decay_sum), 0.0)
    head = jnp.where(segment == 0.0, scale * jnp.exp(decay_sum), 0.0)
    gain = jnp.where(final_seg == 0.0, jnp.exp(last), 0.0)
    rows[DECAY : DECAY + heads, :] = decay_sum
    rows[GATE : GATE + heads, :] = gate
    rows[TAIL : TAIL + heads, :] = tail
    rows[HEAD : HEAD + heads, :] = head
    rows[SEG : SEG + 8, :] = jnp.broadcast_to(segment, (8, width))
    rows[TAIL_GATE : TAIL_GATE + heads, :] = tail * gate
    rows[GAIN : GAIN + heads, :] = jnp.broadcast_to(gain, (heads, width))
    cols[...] = rows[...].T
    for copy in now:
        copy.wait()
    states_of(span, heads, q, k, v, g, cols, rows, send, keep)
    for copy in after:
        copy.wait()


def next_kernel(span, heads, q, k, v, g, cols, rows, send, keep):
    states_of(span, heads, q, k, v, g, cols, rows, send, keep)


def chip_kernel(span, keep, near, rows, *refs):
    through = (len(refs) - 2) // 2
    out, token = refs[through : through + 2]
    token[...] = jnp.zeros_like(token)
    n, width = keep.shape
    m = len(span)
    dk = n // m
    own = rows[GAIN + span[0] : GAIN + span[-1] + 1, 0:LANES]
    for i in range(m):
        at = slice(i * dk, (i + 1) * dk)
        out[at, :] = (keep[at, :] + wide_row(own, i, width) * near[at, :].astype(F32)).astype(BF16)
    out[n:, :] = gain_rows(own * gain_of(near, n, m), width)


def through_kernel(after, x, token, out):
    del after, x, token, out


def far_kernel(m, second, other, first, relayed, token, out):
    n, width = out.shape
    dk = n // m
    gain = gain_of(first, n, m) + gain_of(relayed, n, m)
    for i in range(m):
        at = slice(i * dk, (i + 1) * dk)
        adjacent = first[at, :].astype(F32) + relayed[at, :].astype(F32)
        out[at, :] = (adjacent + wide_row(gain, i, width) * (second[at, :].astype(F32) + other[at, :].astype(F32))).astype(BF16)


def block_kernel(span, heads, scale, q, k, v, g, cols, rows, ready, *refs):
    gq, gk, gv, token = refs[:4] if len(refs) == 4 else refs[1:5]
    token[...] = jnp.zeros_like(token)
    width = q.shape[0]
    half = width // 2
    dk, dv = q.shape[1] // heads, v.shape[1] // heads
    t = lax.broadcasted_iota(jnp.int32, (half, half), 0)
    u = lax.broadcasted_iota(jnp.int32, (half, half), 1)
    causal = t >= u
    spans = [slice(i * half, (i + 1) * half) for i in range(2)]
    seg_c = [cols[s, SEG : SEG + 1] for s in spans]
    seg_r = [rows[SEG : SEG + 1, s] for s in spans]
    pairs = ((0, 0), (1, 0), (1, 1))
    allowed = [(seg_c[a] == seg_r[b]) & causal if a == b else seg_c[a] == seg_r[b] for a, b in pairs]
    for n, h in enumerate(span):
        kk, vv = slice(h * dk, (h + 1) * dk), slice(h * dv, (h + 1) * dv)
        total_q, total_k, total_v = [None] * 2, [None] * 2, [None] * 2

        def add(total, i, x):
            total[i] = x if total[i] is None else total[i] + x

        for (a, b), ok in zip(pairs, allowed, strict=True):
            ra, rb = spans[a], spans[b]
            gap = cols[ra, DECAY + h : DECAY + h + 1] - rows[DECAY + h : DECAY + h + 1, rb]
            decay = scale * jnp.exp(jnp.where(ok, gap, -jnp.inf))
            product = decay * nt(g[ra, vv], v[rb, vv])
            first = (product * rows[GATE + h : GATE + h + 1, rb]).astype(BF16)
            third = (decay * nt(q[ra, kk], k[rb, kk])).astype(BF16)
            add(total_q, a, nn(first, k[rb, kk]))
            add(total_k, b, tn(product.astype(BF16), q[ra, kk]))
            add(total_v, b, tn(third, g[ra, vv]))
        for i in range(2):
            gate = cols[spans[i], GATE + h : GATE + h + 1]
            gq[spans[i], n * dk : (n + 1) * dk] = total_q[i]
            gk[spans[i], n * dk : (n + 1) * dk] = gate * total_k[i]
            gv[spans[i], n * dv : (n + 1) * dv] = gate * total_v[i]


def far_tail_kernel(span, far, k, v, g, cols, gq, gk, gv, *refs):
    out_q, out_k, out_v, buf_q, buf_k, buf_v, sems = refs[-7:]
    even = lax.rem(lax.axis_index("ctx"), 2) == 0
    state = lambda at, width: far[at, :]
    tail_terms(span, even, state, k, v, g, cols, gq, gk, gv, out_q, out_k, out_v, buf_q, buf_k, buf_v, sems)


def near_tail_kernel(span, marks, near, other, far_ready, k, v, g, cols, gq, gk, gv, *refs):
    out_q, out_k, out_v = refs[-7 - marks : -4 - marks]
    buf_q, buf_k, buf_v, sems = refs[-4:]
    for token in refs[-4 - marks : -4]:
        token[...] = jnp.zeros_like(token)
    odd = lax.rem(lax.axis_index("ctx"), 2) == 1
    n, width = other.shape
    gain = gain_of(near, n, len(span))
    dk = n // len(span)

    def state(at, width):
        i = at.start // dk
        return (near[at, :].astype(F32) + wide_row(gain, i, width) * other[at, :].astype(F32)).astype(BF16)

    tail_terms(span, odd, state, k, v, g, cols, gq, gk, gv, out_q, out_k, out_v, buf_q, buf_k, buf_v, sems)


def tail_terms(span, incoming, state, k, v, g, cols, gq, gk, gv, out_q, out_k, out_v, buf_q, buf_k, buf_v, sems):
    m = len(span)
    dk, dv = gk.shape[1] // m, gv.shape[1] // m

    def copy_out(i, h, j):
        src, dst, w = ((buf_q, out_q, dk), (buf_k, out_k, dk), (buf_v, out_v, dv))[j]
        return pltpu.make_async_copy(
            src.at[:, i * w : (i + 1) * w], dst.at[:, h * w : (h + 1) * w], sems.at[i, j]
        )

    def spans_of(i, h):
        return (slice(i * dk, (i + 1) * dk), slice(h * dk, (h + 1) * dk)), (slice(i * dv, (i + 1) * dv), slice(h * dv, (h + 1) * dv))

    @pl.when(incoming)
    def _():
        copies = []
        for i, h in enumerate(span):
            (at, kk), (_, vv) = spans_of(i, h)
            head = cols[:, HEAD + h : HEAD + h + 1]
            buf_q[:, at] = (gq[:, at] + head * nt(g[:, vv], state(at, dv))).astype(BF16)
            copies.append(copy_out(i, h, 0))
            copies[-1].start()
        for copy in copies:
            copy.wait()

    @pl.when(jnp.logical_not(incoming))
    def _():
        copies = []
        for i, h in enumerate(span):
            (at, kk), (bv, vv) = spans_of(i, h)
            tail = cols[:, TAIL_GATE + h : TAIL_GATE + h + 1]
            arriving = state(at, dv)
            buf_v[:, bv] = (gv[:, bv] + tail * nn(k[:, kk], arriving)).astype(BF16)
            copies.append(copy_out(i, h, 2))
            copies[-1].start()
            buf_k[:, at] = (gk[:, at] + tail * nt(v[:, vv], arriving)).astype(BF16)
            copies.append(copy_out(i, h, 1))
            copies[-1].start()
        for copy in copies:
            copy.wait()


def call(kernel, outs, ins, specs_in, specs_out, scratch=(), mib=20, aliases=None):
    return pl.pallas_call(
        kernel,
        out_shape=[jax.ShapeDtypeStruct(*o) for o in outs],
        in_specs=specs_in,
        out_specs=specs_out,
        scratch_shapes=list(scratch),
        input_output_aliases=aliases or {},
        compiler_params=pltpu.CompilerParams(vmem_limit_bytes=mib << 20),
        cost_estimate=pl.CostEstimate(flops=1000, bytes_accessed=1000, transcendentals=0),
    )(*ins)


def in_hbm(x):
    return pltpu.with_memory_space_constraint(x, pltpu.HBM)


def swap(x, route):
    return lax.ppermute(x, "ctx", route)


def routes(size):
    chips = size // 2
    both = lambda pairs: [p for a, b in pairs for p in ((a, b), (b, a))]
    on_chip = both([(2 * c, 2 * c + 1) for c in range(chips)])
    mates = both([(2 * c + 1, 2 * c + 2) for c in range(0, chips, 2)])
    ahead = [(2 * c + 1, 2 * c + 4) for c in range(chips - 2)]
    back = [(2 * c, 2 * c - 3) for c in range(2, chips)]
    feed = ahead[1::2] + back[0::2]
    rest = ahead[0::2] + back[1::2]
    relay = [p for c in range(0, chips, 2) for p in ((2 * c + 2, 2 * c), (2 * c + 1, 2 * c + 3))]
    return on_chip, mates, feed, rest, relay


def body(query_rows, key_rows, value_rows, out_grad, log_forget, input_pre, doc_starts):
    width, heads = log_forget.shape
    dk, dv = query_rows.shape[1] // heads, value_rows.shape[1] // heads
    scale = dk ** (-0.5)
    on_chip, mates, feed, rest, relay = routes(lax.axis_size("ctx"))
    spans, at = [], 0
    for m in CHUNKS:
        spans.append(tuple(range(at, at + m)))
        at += m
    big = tuple(in_hbm(x) for x in (query_rows, key_rows, value_rows, out_grad))
    small = tuple(in_hbm(x) for x in (log_forget.T, input_pre.T, doc_starts.reshape(1, width)))
    mark = ((8, LANES), F32)
    payload = [((m * dk + EXTRA, dv), BF16) for m in CHUNKS]
    total = [((m * dk, dv), F32) for m in CHUNKS]
    send, keep, cols, rows, q, k, v, g = call(
        functools.partial(first_kernel, spans[0], heads, scale),
        [payload[0], total[0], ((width, ROWS), F32), ((ROWS, width), F32)] + [(x.shape, BF16) for x in big],
        small + big,
        [HBM] * 7,
        [VM] * 8,
        [
            pltpu.VMEM((heads, width), F32),
            pltpu.VMEM((heads, width), F32),
            pltpu.VMEM((1, width), jnp.int32),
            pltpu.SemaphoreType.DMA((heads, 4)),
            pltpu.SemaphoreType.DMA((3,)),
        ],
    )
    sends, keeps = [send], [keep]
    for i in range(1, len(CHUNKS)):
        send, keep = call(
            functools.partial(next_kernel, spans[i], heads),
            [payload[i], total[i]],
            (q, k, v, g, cols, rows),
            [VM] * 6,
            [VM] * 2,
        )
        sends.append(send)
        keeps.append(keep)
    nears, firsts, seconds, others, blocks, relayed = [], [], [], [], [], []
    passed = ()
    for i, span in enumerate(spans):
        near = swap(sends[i], on_chip)
        passed = passed + tuple(sends[i + 1 : i + 2])
        count = len(passed)
        chip, token, *passed = call(
            functools.partial(chip_kernel, span),
            [payload[i], mark] + [(x.shape, BF16) for x in passed],
            (keeps[i], near, rows, *passed),
            [VM] * (3 + count),
            [VM] * (2 + count),
            mib=8,
            aliases={3 + j: 2 + j for j in range(count)},
        )
        seconds.append(swap(chip, feed))
        others.append(swap(chip, rest))
        if i + 1 < len(spans):
            sends[i + 1] = passed[-1]
        passed = ()
        firsts.append(swap(chip, mates))
        nears.append(near)
    marks = [token]
    passed = ()
    for i, span in enumerate(spans):
        m = len(span)
        count = len(passed)
        *block, token, = call(
            functools.partial(block_kernel, span, heads, scale),
            [((width, m * dk), F32), ((width, m * dk), F32), ((width, m * dv), F32), mark]
            + [(x.shape, BF16) for x in passed],
            (q, k, v, g, cols, rows, token, *passed),
            [VM] * (7 + count),
            [VM] * (4 + count),
            aliases={7 + j: 4 + j for j in range(count)},
        )
        blocks.append(block)
        marks.append(token)
    for i, ready in enumerate((marks[0], marks[1])):
        (seconds[i],) = call(
            through_kernel, payload[i : i + 1], (firsts[i], seconds[i], ready), [VM] * 3, [VM], mib=8, aliases={1: 0}
        )
        relayed.append(swap(seconds[i], relay))
    outs = ()
    shapes = [(query_rows.shape, BF16), (key_rows.shape, BF16), (value_rows.shape, BF16)]
    for i, span in enumerate(spans):
        m = len(span)
        (far,) = call(
            functools.partial(far_kernel, m),
            [((m * dk, dv), BF16)],
            (seconds[i], others[i], firsts[i], relayed[i], token),
            [VM] * 5,
            [VM],
            mib=8,
        )
        other = swap(far, on_chip)
        scratch = [
            pltpu.VMEM((width, m * dk), BF16),
            pltpu.VMEM((width, m * dk), BF16),
            pltpu.VMEM((width, m * dv), BF16),
            pltpu.SemaphoreType.DMA((m, 3)),
        ]
        outs = call(
            functools.partial(far_tail_kernel, span),
            shapes,
            (far, k, v, g, cols, *blocks[i]) + tuple(in_hbm(x) for x in outs),
            [VM] * 8 + [HBM] * len(outs),
            [HBM] * 3,
            scratch,
            aliases={8 + j: j for j in range(len(outs))},
        )
        marks = int(i + 1 < len(spans))
        outs = call(
            functools.partial(near_tail_kernel, span, marks),
            shapes + [mark] * marks,
            (nears[i], other, far, k, v, g, cols, *blocks[i]) + tuple(in_hbm(x) for x in outs),
            [VM] * 10 + [HBM] * len(outs),
            [HBM] * 3 + [VM] * marks,
            scratch,
            aliases={10 + j: j for j in range(len(outs))},
        )
        token, outs = outs[-1], outs[:3]
    return tuple(outs)


def solution(mesh):
    row = P(("groups", "ctx"), None)
    in_specs = (row,) * 6 + (P(("groups", "ctx")),)
    return jax.shard_map(body, mesh=mesh, in_specs=in_specs, out_specs=(row,) * 3, check_vma=False)
```

```python
import functools

import jax
import jax.numpy as jnp
from jax import lax
from jax.experimental import pallas as pl
from jax.experimental.pallas import tpu as pltpu
from jax.sharding import PartitionSpec as P

F32 = jnp.float32
BF16 = jnp.bfloat16
LANES = 128
EXTRA = 8
CHUNKS = (2, 2)
DECAY, GATE, TAIL, HEAD, SEG, TAIL_GATE, GAIN, ROWS = 0, 4, 8, 12, 16, 24, 28, 32
VM = pl.BlockSpec(memory_space=pltpu.VMEM)
HBM = pl.BlockSpec(memory_space=pltpu.HBM)


def nt(a, b):
    return lax.dot_general(a, b, (((1,), (1,)), ((), ())), preferred_element_type=F32)


def nn(a, b):
    return lax.dot_general(a, b, (((1,), (0,)), ((), ())), preferred_element_type=F32)


def tn(a, b):
    return lax.dot_general(a, b, (((0,), (0,)), ((), ())), preferred_element_type=F32)


def three_terms(x):
    hi = x.astype(BF16)
    rest = x - hi.astype(F32)
    mid = rest.astype(BF16)
    lo = (rest - mid.astype(F32)).astype(BF16)
    return hi, mid, lo


def running_sums(x):
    rows, width = x.shape
    cuts = width // LANES
    stack = jnp.concatenate([x[:, i * LANES : (i + 1) * LANES] for i in range(cuts)], axis=0)
    parts = jnp.concatenate([t.astype(F32) for t in three_terms(stack)], axis=0).astype(BF16)
    earlier = lax.broadcasted_iota(jnp.int32, (LANES, LANES), 0)
    later = lax.broadcasted_iota(jnp.int32, (LANES, LANES), 1)
    upper = jnp.where(earlier <= later, 1.0, 0.0).astype(BF16)
    sums = nn(parts, upper)
    m = rows * cuts
    sums = sums[:m] + sums[m : 2 * m] + sums[2 * m :]
    pieces, base = [], jnp.zeros((rows, 1), F32)
    for i in range(cuts):
        piece = sums[i * rows : (i + 1) * rows]
        pieces.append(piece + base)
        base = base + piece[:, LANES - 1 :]
    return jnp.concatenate(pieces, axis=1)


def gain_rows(gain, width):
    wide = [jnp.broadcast_to(gain[i : i + 1], (EXTRA, LANES)) for i in range(gain.shape[0])]
    wide = jnp.concatenate(wide + [jnp.zeros((EXTRA, width - LANES * len(wide)), F32)], axis=1)
    hi, mid, lo = (t.astype(F32) for t in three_terms(wide))
    row = lax.broadcasted_iota(jnp.int32, wide.shape, 0)
    out = jnp.where(row == 0, hi, jnp.where(row == 1, mid, jnp.where(row == 2, lo, 0.0)))
    return out.astype(BF16)


def gain_of(ref, at, heads):
    block = ref[at : at + EXTRA, :].astype(F32)
    total = block[0:1] + block[1:2] + block[2:3]
    return jnp.concatenate([total[:, h * LANES : (h + 1) * LANES] for h in range(heads)], axis=0)


def wide_row(gain, h, width):
    return jnp.concatenate([gain[h : h + 1]] * (width // LANES), axis=1)


def states_of(span, heads, q, k, v, g, cols, rows, send, keep):
    dk, dv = q.shape[1] // heads, v.shape[1] // heads
    even = lax.rem(lax.axis_index("ctx"), 2) == 0
    for i, h in enumerate(span):
        kk, vv, at = slice(h * dk, (h + 1) * dk), slice(h * dv, (h + 1) * dv), slice(i * dk, (i + 1) * dk)
        scaled_v = (cols[:, TAIL_GATE + h : TAIL_GATE + h + 1] * v[:, vv].astype(F32)).astype(BF16)
        scaled_q = (cols[:, HEAD + h : HEAD + h + 1] * q[:, kk].astype(F32)).astype(BF16)
        forward = tn(k[:, kk], scaled_v)
        backward = tn(scaled_q, g[:, vv])
        send[at, :] = jnp.where(even, forward, backward).astype(BF16)
        keep[at, :] = jnp.where(even, backward, forward)
    send[len(span) * dk :, :] = gain_rows(rows[GAIN + span[0] : GAIN + span[-1] + 1, 0:LANES], dv)


def first_kernel(
    span, heads, scale, lf_in, ip_in, st_in, q_in, k_in, v_in, g_in, send, keep, cols, rows, q, k, v, g, lf, ip, st, sems, small
):
    width = q.shape[0]
    dk, dv = q.shape[1] // heads, v.shape[1] // heads
    gates = [pltpu.make_async_copy(x, y, small.at[i]) for i, (x, y) in enumerate(((lf_in, lf), (ip_in, ip), (st_in, st)))]
    for copy in gates:
        copy.start()
    copies = []
    for h in range(heads):
        for i, (src, dst, w) in enumerate(((k_in, k, dk), (v_in, v, dv), (q_in, q, dk), (g_in, g, dv))):
            at = pl.ds(h * w, w)
            copies.append(pltpu.make_async_copy(src.at[:, at], dst.at[:, at], sems.at[h, i]))
    now, after = copies[: 4 * len(span)], copies[4 * len(span) :]
    for copy in now:
        copy.start()
    for copy in gates:
        copy.wait()
    for copy in after:
        copy.start()
    filler = jnp.zeros((7 - heads, width), F32)
    sums = running_sums(jnp.concatenate([lf[...], st[...].astype(F32), filler], axis=0))
    decay_sum, segment = sums[0:heads], sums[heads : heads + 1]
    last, final_seg = decay_sum[:, width - 1 :], segment[:, width - 1 :]
    gate = jnp.exp(ip[...])
    tail = jnp.where(segment == final_seg, jnp.exp(last - decay_sum), 0.0)
    head = jnp.where(segment == 0.0, scale * jnp.exp(decay_sum), 0.0)
    gain = jnp.where(final_seg == 0.0, jnp.exp(last), 0.0)
    rows[DECAY : DECAY + heads, :] = decay_sum
    rows[GATE : GATE + heads, :] = gate
    rows[TAIL : TAIL + heads, :] = tail
    rows[HEAD : HEAD + heads, :] = head
    rows[SEG : SEG + 8, :] = jnp.broadcast_to(segment, (8, width))
    rows[TAIL_GATE : TAIL_GATE + heads, :] = tail * gate
    rows[GAIN : GAIN + heads, :] = jnp.broadcast_to(gain, (heads, width))
    cols[...] = rows[...].T
    for copy in now:
        copy.wait()
    states_of(span, heads, q, k, v, g, cols, rows, send, keep)
    for copy in after:
        copy.wait()


def next_kernel(span, heads, q, k, v, g, cols, rows, send, keep):
    states_of(span, heads, q, k, v, g, cols, rows, send, keep)


def chip_kernel(span, keep, near, rows, *refs):
    through = (len(refs) - 2) // 2
    out, token = refs[through : through + 2]
    token[...] = jnp.zeros_like(token)
    n, width = keep.shape
    m = len(span)
    dk = n // m
    own = rows[GAIN + span[0] : GAIN + span[-1] + 1, 0:LANES]
    for i in range(m):
        at = slice(i * dk, (i + 1) * dk)
        out[at, :] = (keep[at, :] + wide_row(own, i, width) * near[at, :].astype(F32)).astype(BF16)
    out[n:, :] = gain_rows(own * gain_of(near, n, m), width)


def through_kernel(after, x, token, out):
    del after, x, token, out


def far_kernel(m, relayed, second, first, other, token, out):
    n, width = out.shape
    dk = n // m
    gain = gain_of(first, n, m) + gain_of(relayed, n, m)
    for i in range(m):
        at = slice(i * dk, (i + 1) * dk)
        adjacent = first[at, :].astype(F32) + relayed[at, :].astype(F32)
        out[at, :] = (adjacent + wide_row(gain, i, width) * (second[at, :].astype(F32) + other[at, :].astype(F32))).astype(BF16)


def block_kernel(span, heads, scale, q, k, v, g, cols, rows, ready, *refs):
    gq, gk, gv, token = refs[:4] if len(refs) == 4 else refs[1:5]
    token[...] = jnp.zeros_like(token)
    width = q.shape[0]
    half = width // 2
    dk, dv = q.shape[1] // heads, v.shape[1] // heads
    t = lax.broadcasted_iota(jnp.int32, (half, half), 0)
    u = lax.broadcasted_iota(jnp.int32, (half, half), 1)
    causal = t >= u
    spans = [slice(i * half, (i + 1) * half) for i in range(2)]
    seg_c = [cols[s, SEG : SEG + 1] for s in spans]
    seg_r = [rows[SEG : SEG + 1, s] for s in spans]
    pairs = ((0, 0), (1, 0), (1, 1))
    allowed = [(seg_c[a] == seg_r[b]) & causal if a == b else seg_c[a] == seg_r[b] for a, b in pairs]
    for n, h in enumerate(span):
        kk, vv = slice(h * dk, (h + 1) * dk), slice(h * dv, (h + 1) * dv)
        total_q, total_k, total_v = [None] * 2, [None] * 2, [None] * 2

        def add(total, i, x):
            total[i] = x if total[i] is None else total[i] + x

        for (a, b), ok in zip(pairs, allowed, strict=True):
            ra, rb = spans[a], spans[b]
            gap = cols[ra, DECAY + h : DECAY + h + 1] - rows[DECAY + h : DECAY + h + 1, rb]
            decay = scale * jnp.exp(jnp.where(ok, gap, -jnp.inf))
            product = decay * nt(g[ra, vv], v[rb, vv])
            first = (product * rows[GATE + h : GATE + h + 1, rb]).astype(BF16)
            third = (decay * nt(q[ra, kk], k[rb, kk])).astype(BF16)
            add(total_q, a, nn(first, k[rb, kk]))
            add(total_k, b, tn(product.astype(BF16), q[ra, kk]))
            add(total_v, b, tn(third, g[ra, vv]))
        for i in range(2):
            gate = cols[spans[i], GATE + h : GATE + h + 1]
            gq[spans[i], n * dk : (n + 1) * dk] = total_q[i]
            gk[spans[i], n * dk : (n + 1) * dk] = gate * total_k[i]
            gv[spans[i], n * dv : (n + 1) * dv] = gate * total_v[i]


def far_tail_kernel(span, far, k, v, g, cols, gq, gk, gv, *refs):
    out_q, out_k, out_v, buf_q, buf_k, buf_v, sems = refs[-7:]
    even = lax.rem(lax.axis_index("ctx"), 2) == 0
    state = lambda at, width: far[at, :]
    tail_terms(span, even, state, k, v, g, cols, gq, gk, gv, out_q, out_k, out_v, buf_q, buf_k, buf_v, sems)


def near_tail_kernel(span, marks, near, other, far_ready, k, v, g, cols, gq, gk, gv, *refs):
    out_q, out_k, out_v = refs[-7 - marks : -4 - marks]
    buf_q, buf_k, buf_v, sems = refs[-4:]
    for token in refs[-4 - marks : -4]:
        token[...] = jnp.zeros_like(token)
    odd = lax.rem(lax.axis_index("ctx"), 2) == 1
    n, width = other.shape
    gain = gain_of(near, n, len(span))
    dk = n // len(span)

    def state(at, width):
        i = at.start // dk
        return (near[at, :].astype(F32) + wide_row(gain, i, width) * other[at, :].astype(F32)).astype(BF16)

    tail_terms(span, odd, state, k, v, g, cols, gq, gk, gv, out_q, out_k, out_v, buf_q, buf_k, buf_v, sems)


def tail_terms(span, incoming, state, k, v, g, cols, gq, gk, gv, out_q, out_k, out_v, buf_q, buf_k, buf_v, sems):
    m = len(span)
    dk, dv = gk.shape[1] // m, gv.shape[1] // m

    def copy_out(i, h, j):
        src, dst, w = ((buf_q, out_q, dk), (buf_k, out_k, dk), (buf_v, out_v, dv))[j]
        return pltpu.make_async_copy(
            src.at[:, i * w : (i + 1) * w], dst.at[:, h * w : (h + 1) * w], sems.at[i, j]
        )

    def spans_of(i, h):
        return (slice(i * dk, (i + 1) * dk), slice(h * dk, (h + 1) * dk)), (slice(i * dv, (i + 1) * dv), slice(h * dv, (h + 1) * dv))

    @pl.when(incoming)
    def _():
        copies = []
        for i, h in enumerate(span):
            (at, kk), (_, vv) = spans_of(i, h)
            head = cols[:, HEAD + h : HEAD + h + 1]
            buf_q[:, at] = (gq[:, at] + head * nt(g[:, vv], state(at, dv))).astype(BF16)
            copies.append(copy_out(i, h, 0))
            copies[-1].start()
        for copy in copies:
            copy.wait()

    @pl.when(jnp.logical_not(incoming))
    def _():
        copies = []
        for i, h in enumerate(span):
            (at, kk), (bv, vv) = spans_of(i, h)
            tail = cols[:, TAIL_GATE + h : TAIL_GATE + h + 1]
            arriving = state(at, dv)
            buf_v[:, bv] = (gv[:, bv] + tail * nn(k[:, kk], arriving)).astype(BF16)
            copies.append(copy_out(i, h, 2))
            copies[-1].start()
            buf_k[:, at] = (gk[:, at] + tail * nt(v[:, vv], arriving)).astype(BF16)
            copies.append(copy_out(i, h, 1))
            copies[-1].start()
        for copy in copies:
            copy.wait()


def call(kernel, outs, ins, specs_in, specs_out, scratch=(), mib=20, aliases=None):
    return pl.pallas_call(
        kernel,
        out_shape=[jax.ShapeDtypeStruct(*o) for o in outs],
        in_specs=specs_in,
        out_specs=specs_out,
        scratch_shapes=list(scratch),
        input_output_aliases=aliases or {},
        compiler_params=pltpu.CompilerParams(vmem_limit_bytes=mib << 20),
        cost_estimate=pl.CostEstimate(flops=1000, bytes_accessed=1000, transcendentals=0),
    )(*ins)


def in_hbm(x):
    return pltpu.with_memory_space_constraint(x, pltpu.HBM)


def swap(x, route):
    return lax.ppermute(x, "ctx", route)


def routes(size):
    chips = size // 2
    both = lambda pairs: [p for a, b in pairs for p in ((a, b), (b, a))]
    on_chip = both([(2 * c, 2 * c + 1) for c in range(chips)])
    mates = both([(2 * c + 1, 2 * c + 2) for c in range(0, chips, 2)])
    ahead = [(2 * c + 1, 2 * c + 4) for c in range(chips - 2)]
    back = [(2 * c, 2 * c - 3) for c in range(2, chips)]
    feed = ahead[1::2] + back[0::2]
    rest = ahead[0::2] + back[1::2]
    relay = [p for c in range(0, chips, 2) for p in ((2 * c + 2, 2 * c), (2 * c + 1, 2 * c + 3))]
    return on_chip, mates, feed, rest, relay


def body(query_rows, key_rows, value_rows, out_grad, log_forget, input_pre, doc_starts):
    width, heads = log_forget.shape
    dk, dv = query_rows.shape[1] // heads, value_rows.shape[1] // heads
    scale = dk ** (-0.5)
    on_chip, mates, feed, rest, relay = routes(lax.axis_size("ctx"))
    spans, at = [], 0
    for m in CHUNKS:
        spans.append(tuple(range(at, at + m)))
        at += m
    big = tuple(in_hbm(x) for x in (query_rows, key_rows, value_rows, out_grad))
    small = tuple(in_hbm(x) for x in (log_forget.T, input_pre.T, doc_starts.reshape(1, width)))
    mark = ((8, LANES), F32)
    payload = [((m * dk + EXTRA, dv), BF16) for m in CHUNKS]
    total = [((m * dk, dv), F32) for m in CHUNKS]
    send, keep, cols, rows, q, k, v, g = call(
        functools.partial(first_kernel, spans[0], heads, scale),
        [payload[0], total[0], ((width, ROWS), F32), ((ROWS, width), F32)] + [(x.shape, BF16) for x in big],
        small + big,
        [HBM] * 7,
        [VM] * 8,
        [
            pltpu.VMEM((heads, width), F32),
            pltpu.VMEM((heads, width), F32),
            pltpu.VMEM((1, width), jnp.int32),
            pltpu.SemaphoreType.DMA((heads, 4)),
            pltpu.SemaphoreType.DMA((3,)),
        ],
    )
    sends, keeps = [send], [keep]
    for i in range(1, len(CHUNKS)):
        send, keep = call(
            functools.partial(next_kernel, spans[i], heads),
            [payload[i], total[i]],
            (q, k, v, g, cols, rows),
            [VM] * 6,
            [VM] * 2,
        )
        sends.append(send)
        keeps.append(keep)
    nears, firsts, seconds, others, blocks, relayed = [], [], [], [], [], []
    passed = ()
    for i, span in enumerate(spans):
        near = swap(sends[i], on_chip)
        passed = passed + tuple(sends[i + 1 : i + 2])
        count = len(passed)
        chip, token, *passed = call(
            functools.partial(chip_kernel, span),
            [payload[i], mark] + [(x.shape, BF16) for x in passed],
            (keeps[i], near, rows, *passed),
            [VM] * (3 + count),
            [VM] * (2 + count),
            mib=8,
            aliases={3 + j: 2 + j for j in range(count)},
        )
        seconds.append(swap(chip, feed))
        others.append(swap(chip, rest))
        if i + 1 < len(spans):
            sends[i + 1] = passed[-1]
        passed = ()
        firsts.append(swap(chip, mates))
        nears.append(near)
    marks = [token]
    passed = ()
    for i, span in enumerate(spans):
        m = len(span)
        count = len(passed)
        *block, token, = call(
            functools.partial(block_kernel, span, heads, scale),
            [((width, m * dk), F32), ((width, m * dk), F32), ((width, m * dv), F32), mark]
            + [(x.shape, BF16) for x in passed],
            (q, k, v, g, cols, rows, token, *passed),
            [VM] * (7 + count),
            [VM] * (4 + count),
            aliases={7 + j: 4 + j for j in range(count)},
        )
        blocks.append(block)
        marks.append(token)
    for i, ready in enumerate((marks[0], marks[1])):
        (seconds[i],) = call(
            through_kernel, payload[i : i + 1], (firsts[i], seconds[i], ready), [VM] * 3, [VM], mib=8, aliases={1: 0}
        )
        relayed.append(swap(seconds[i], relay))
    outs = ()
    shapes = [(query_rows.shape, BF16), (key_rows.shape, BF16), (value_rows.shape, BF16)]
    for i, span in enumerate(spans):
        m = len(span)
        (far,) = call(
            functools.partial(far_kernel, m),
            [((m * dk, dv), BF16)],
            (relayed[i], seconds[i], firsts[i], others[i], token),
            [VM] * 5,
            [VM],
            mib=8,
        )
        other = swap(far, on_chip)
        scratch = [
            pltpu.VMEM((width, m * dk), BF16),
            pltpu.VMEM((width, m * dk), BF16),
            pltpu.VMEM((width, m * dv), BF16),
            pltpu.SemaphoreType.DMA((m, 3)),
        ]
        outs = call(
            functools.partial(far_tail_kernel, span),
            shapes,
            (far, k, v, g, cols, *blocks[i]) + tuple(in_hbm(x) for x in outs),
            [VM] * 8 + [HBM] * len(outs),
            [HBM] * 3,
            scratch,
            aliases={8 + j: j for j in range(len(outs))},
        )
        marks = int(i + 1 < len(spans))
        outs = call(
            functools.partial(near_tail_kernel, span, marks),
            shapes + [mark] * marks,
            (nears[i], other, far, k, v, g, cols, *blocks[i]) + tuple(in_hbm(x) for x in outs),
            [VM] * 10 + [HBM] * len(outs),
            [HBM] * 3 + [VM] * marks,
            scratch,
            aliases={10 + j: j for j in range(len(outs))},
        )
        token, outs = outs[-1], outs[:3]
    return tuple(outs)


def solution(mesh):
    row = P(("groups", "ctx"), None)
    in_specs = (row,) * 6 + (P(("groups", "ctx")),)
    return jax.shard_map(body, mesh=mesh, in_specs=in_specs, out_specs=(row,) * 3, check_vma=False)
```
